128 devices in a mesh: blk: 16 (over z_hi, x, core), head: 8 (over y, z_lo).
Axes of the slice: x: 4, y: 4, z: 4 (z_hi: 2, z_lo: 2; z = z_hi * 2 + z_lo), core: 2. Of those that a mesh axis runs over, the one named last changes fastest.
Arguments:
- queries: bfloat16 [8192, 8192], P('blk', 'head'), may hold values from -120 to 120
- keys: bfloat16 [8192, 1024], P('blk', 'head'), may hold values from -6.5 to 6.5
- values: bfloat16 [8192, 1024], P('blk', 'head'), may hold values from -6 to 6
- w_out: bfloat16 [8192, 8192], P('head'), may hold values from -0.09375 to 0.09375
- order: int32 [32], replicated, may hold values from 0 to 31, each once
Outputs:
- mixed: bfloat16 [8192, 8192], P('blk', 'head')
The draws below stay inside these ranges and needn't reach their ends.
Inputs may be any that keep to these rules, and one draw needn't show every extreme that they name: `order`: A permutation of 0 to 31.
All inputs are finite; a program needn't handle non-finite values.
Results may differ from the reference program's by a relative error of at most 0.015.
Values may be sent and summed in bfloat16 or wider, within the bound.
A program may use at most 128 MiB of HBM per device.

```python
import math
import jax
import jax.numpy as jnp
from jax import lax

D = 8192
H = 64
KVH = 8
HD = 128
TOK_DEV = 512
SEQ = 8192
BLOCKS = 32


def draw_keys(key, part):
    drawn = jnp.clip(jax.random.normal(jax.random.fold_in(key, 13), (SEQ, KVH * HD), jnp.float32), -6.0, 6.0)
    return drawn.astype(jnp.bfloat16)


def draw_queries(key, part):
    drawn = jnp.clip(jax.random.normal(jax.random.fold_in(key, 31), (SEQ, H * HD), jnp.float32), -6.0, 6.0)
    return drawn.astype(jnp.bfloat16)


def with_spikes(array, rng, source, target, parts, factor):
    owner, partner = [(jnp.arange(array.shape[dim]) // (array.shape[dim] // parts)).reshape([-1 if axis == dim else 1 for axis in range(array.ndim)]) for dim in (source, target)]
    chosen = jax.random.permutation(rng, parts)[partner]
    strong = (owner == chosen) | (owner == (partner + parts // 2) % parts)
    return jnp.where(strong, factor * array, array)


def levels(own_key, extent, cuts, smallest, largest):
    gain = 1.0
    for axis_at, parts in cuts:
        draws = jax.random.uniform(jax.random.fold_in(jax.random.fold_in(own_key, 6), axis_at), (parts,), jnp.float32, smallest / len(cuts), largest / len(cuts))
        gain = gain * jnp.repeat(jnp.exp(draws), extent[axis_at] // parts).reshape((-1,) + (1,) * (len(extent) - 1 - axis_at))
    return gain


def normal_values(stream_key, dims, scale, most, cuts=(), kind=jnp.bfloat16):
    entries = scale * jax.random.normal(stream_key, dims, jnp.float32)
    if cuts:
        entries = entries * levels(stream_key, dims, cuts, -0.22, 0.18)
    return jnp.clip(entries, -most, most).astype(kind)


def gaussian_with(own_key, dims, deviation, reach, shards, heavy, kind=jnp.bfloat16):
    values = deviation * jax.random.normal(own_key, dims, jnp.float32)
    if shards:
        values = values * levels(own_key, dims, shards, -0.22, 0.18)
    return jnp.clip(with_spikes(values, jax.random.fold_in(own_key, 3), *heavy), -reach, reach).astype(kind)


def setup_inputs(seed: int = 0) -> dict:
    key_list = jax.random.split(jax.random.key(seed), 6)
    queries = draw_queries(jax.random.fold_in(key_list[5], 71), 0)
    keys = draw_keys(jax.random.fold_in(key_list[5], 71), 0)
    values = normal_values(key_list[2], (SEQ, KVH * HD), 1.0, 6.0, ((0, 16), (1, 8)))
    w_out = gaussian_with(key_list[3], (H * HD, D), (H * HD) ** -0.5, 0.09375, ((0, 8),), (0, 1, 8, 2.0))
    order = jax.random.permutation(key_list[4], BLOCKS).astype(jnp.int32)
    return {"queries": queries, "keys": keys, "values": values, "w_out": w_out, "order": order}


def reference(queries, keys, values, w_out, order):
    seq = queries.shape[0]
    half = TOK_DEV // 2
    group = H // KVH
    scale = HD ** -0.5
    rows = jnp.arange(seq, dtype=jnp.int32)
    position = (order[rows // half] * half + rows % half).astype(jnp.int32)
    qb = math.gcd(seq, 512)
    nq = seq // qb
    q_all = queries.reshape(nq, qb, KVH, group, HD)
    k_all = keys.reshape(seq, KVH, HD)
    v_all = values.reshape(seq, KVH, HD)
    qpos_all = position.reshape(nq, qb)

    def per_head(kv_index):
        k_head = lax.dynamic_index_in_dim(k_all, kv_index, 1, keepdims=False).astype(jnp.float32)
        v_head = lax.dynamic_index_in_dim(v_all, kv_index, 1, keepdims=False).astype(jnp.float32)

        def per_block(block):
            q_block = lax.dynamic_index_in_dim(q_all[block], kv_index, 1, keepdims=False).astype(jnp.float32)
            qpos = qpos_all[block]
            score = jnp.einsum("tgd,nd->tgn", q_block, k_head) * scale
            visible = position[None, None, :] <= qpos[:, None, None]
            score = jnp.where(visible, score, -1e30)
            top = jnp.max(score, axis=-1, keepdims=True)
            weight = jnp.where(visible, jnp.exp(score - top), 0.0)
            total = jnp.sum(weight, axis=-1)
            weight_low = weight.astype(jnp.bfloat16).astype(jnp.float32)
            summed = jnp.einsum("tgn,nd->tgd", weight_low, v_head)
            return (summed / total[:, :, None]).astype(jnp.bfloat16)

        return lax.map(per_block, jnp.arange(nq))

    heads = lax.map(per_head, jnp.arange(KVH))
    attended = jnp.transpose(heads, (1, 2, 0, 3, 4)).reshape(seq, H * HD)
    return jnp.dot(attended, w_out, preferred_element_type=jnp.float32).astype(jnp.bfloat16)
```

```python
import jax
import jax.numpy as jnp
from jax import lax
from jax.experimental import pallas as pl
from jax.experimental.pallas import tpu as pltpu
from jax.sharding import PartitionSpec as P

HD = 128
CHUNK = 128
CHUNKS = 4
HEADS = 8
SUBS = 4
ZCOLS = 384
YCOLS = 640
SCALE2 = HD**-0.5 * 1.4426950408889634
HIDDEN = -1e30
MESH = pl.DeviceIdType.MESH
BF = jnp.bfloat16
F32 = jnp.float32
FAR, NEAR, ZSUM, ZPRE, ZFAR, ZNEAR = 0, 2, 6, 7, 8, 10


def mod(a, n):
    return lax.rem(a, n)


def div(a, n):
    return lax.div(a, n)


def kernel(
    order, q, k, v, w_hbm, out,
    kv, w, eye, masks, top, acc, att,
    py, pz, far, near, zsum, zpre, zfar, znear,
    kv_send, kv_recv, send, recv, w_sem,
):
    blk = lax.axis_index("blk")
    head = lax.axis_index("head")
    core = mod(blk, 2)
    x = mod(div(blk, 2), 4)
    zh = div(blk, 8)
    y = div(head, 2)
    zl = mod(head, 2)

    def block(dz, dx):
        return (mod(zh + dz, 2) * 4 + mod(x + dx, 4)) * 2 + core

    left, right, across = block(0, 3), block(0, 1), block(1, 0)
    mate = blk + 1 - 2 * core
    up = mod(y + 1, 4) * 2 + zl
    down = mod(y + 3, 4) * 2 + zl
    zmate = head + 1 - 2 * zl

    barrier = pltpu.get_barrier_semaphore()
    for peer in (left, right, across, mate):
        pl.semaphore_signal(barrier, inc=1, device_id=(peer, head), device_id_type=MESH)
    for peer in (up, down, zmate):
        pl.semaphore_signal(barrier, inc=1, device_id=(blk, peer), device_id_type=MESH)
    pl.semaphore_wait(barrier, 7)

    w_copy = pltpu.make_async_copy(w_hbm, w, w_sem)

    kv_sends = []

    def pass_on(source, part, to, own=False):
        ref = (k, v)[part] if own else kv.at[source, part]
        copy = pltpu.make_async_remote_copy(
            src_ref=ref, dst_ref=kv.at[source, part],
            send_sem=kv_send.at[len(kv_sends)], recv_sem=kv_recv.at[source, part],
            device_id=(to, head), device_id_type=MESH,
        )
        kv_sends.append(0)
        copy.start()

    def arrived(source, part):
        pltpu.make_async_remote_copy(
            src_ref=kv.at[source, part], dst_ref=kv.at[source, part],
            send_sem=kv_send.at[0], recv_sem=kv_recv.at[source, part],
            device_id=(mate, head), device_id_type=MESH,
        ).wait_recv()

    def mate_has(dz, dx):
        source = block(dz, dx) + 1 - 2 * core
        arrived(source, 0)
        arrived(source, 1)

    for to in (across, right, left, mate):
        for part in (0, 1):
            pass_on(blk, part, to, own=True)
    w_copy.start()

    kv[blk, 0] = k[...]
    kv[blk, 1] = v[...]
    row = lax.broadcasted_iota(jnp.int32, (128, 128), 0)
    col = lax.broadcasted_iota(jnp.int32, (128, 128), 1)
    eye[...] = jnp.where(row == col, 1.0, 0.0).astype(BF)
    masks[0] = jnp.zeros((128, 128), BF)
    masks[1] = jnp.where(row > col, HIDDEN, 0.0).astype(BF)
    masks[2] = jnp.full((128, 128), HIDDEN, BF)

    def gather_0():
        arrived(left, 0)
        pass_on(left, 0, right)
        arrived(right, 1)
        pass_on(right, 1, left)
        arrived(right, 0)
        arrived(left, 1)
        for part in (0, 1):
            pass_on(right, part, mate)
        for part in (0, 1):
            pass_on(left, part, mate)
        for part in (0, 1):
            arrived(across, part)
            pass_on(across, part, right)
            pass_on(across, part, left)
        for part in (0, 1):
            pass_on(across, part, mate)
        mate_has(0, 0)
        mate_has(0, 1)

    def gather_1():
        far_block = block(0, 2)
        for part in (0, 1):
            arrived(far_block, part)
            pass_on(far_block, part, mate)
        mate_has(0, 3)
        mate_has(1, 0)

    def gather_2():
        zleft, zright = block(1, 3), block(1, 1)
        arrived(zleft, 0)
        pass_on(zleft, 0, right)
        arrived(zright, 1)
        pass_on(zright, 1, left)
        arrived(zleft, 1)
        arrived(zright, 0)
        for source in (zleft, zright):
            for part in (0, 1):
                pass_on(source, part, mate)
        mate_has(0, 2)
        mate_has(1, 3)

    def gather_3():
        zfar_block = block(1, 2)
        for part in (0, 1):
            arrived(zfar_block, part)
            pass_on(zfar_block, part, mate)
        mate_has(1, 1)
        mate_has(1, 2)

    def attend(c, s):
        rows = pl.ds(pl.multiple_of(c * CHUNK, CHUNK), CHUNK)
        query_pos = 2 * order[2 * blk + div(c, 2)] + mod(c, 2)
        chips = (
            mod(zh + div(s, 3), 2) * 4 + mod(x + 4 - s, 4),
            mod(zh + div(s + 2, 3), 2) * 4 + mod(x + 5 - s, 4),
        )
        key_rows, value_rows = [], []
        ones = jnp.ones((128, 128), BF)
        for chip in chips:
            for b in (2 * chip, 2 * chip + 1):
                for t in range(4):
                    key_pos = 2 * order[2 * b + t // 2] + t % 2
                    kind = (key_pos > query_pos).astype(jnp.int32) + (
                        key_pos >= query_pos
                    ).astype(jnp.int32)
                    part = slice(t * 128, (t + 1) * 128)
                    key_rows.append(jnp.concatenate([kv[b, 0, part, :], masks[kind]], axis=1))
                    value_rows.append(jnp.concatenate([kv[b, 1, part, :], ones], axis=1))
        key_tile = jnp.concatenate(key_rows, axis=0)
        value_tile = jnp.concatenate(value_rows, axis=0)
        for u in range(SUBS):
            q_rows = [
                jnp.concatenate([q[rows, h * HD : (h + 1) * HD], eye[...]], axis=1)
                for h in (2 * u, 2 * u + 1)
            ]
            score = lax.dot_general(
                jnp.concatenate(q_rows, axis=0), key_tile,
                (((1,), (1,)), ((), ())), preferred_element_type=F32,
            )
            old = top[u]
            new = jnp.maximum(old, jnp.max(score, axis=1, keepdims=True) * SCALE2)
            weight = jnp.exp2(score * SCALE2 - new).astype(BF)
            acc[u] = acc[u] * jnp.exp2(old - new) + jnp.dot(
                weight, value_tile, preferred_element_type=F32
            )
            top[u] = new

    def start_chunk():
        top[...] = jnp.full_like(top, HIDDEN)
        acc[...] = jnp.zeros_like(acc)

    def project(c):
        for u in range(SUBS):
            mean = (acc[u, :, :HD] / acc[u, :, HD:]).astype(BF)
            for h in range(2):
                at = (2 * u + h) * HD
                att[:, at : at + HD] = mean[h * CHUNK : (h + 1) * CHUNK]

        def one(i, _):
            to_y = mod(y + 2 + div(i, 2), 4)
            to_z = mod(i, 2)
            columns = pl.ds(pl.multiple_of((to_y * 2 + to_z) * 1024, 1024), 1024)
            part = jnp.dot(att[...], w[:, columns], preferred_element_type=F32).astype(BF)
            pz[c, to_z * 4 + to_y] = part[:, :ZCOLS]
            py[c, to_z * 4 + to_y] = part[:, ZCOLS:]
            return 0

        lax.fori_loop(0, 8, one, 0)

    def to_y(src, dst, c, n, peer):
        return pltpu.make_async_remote_copy(
            src_ref=src, dst_ref=dst, send_sem=send.at[c, n], recv_sem=recv.at[c, n],
            device_id=(blk, peer), device_id_type=MESH,
        )

    y_up, y_down, y_far = mod(y + 1, 4), mod(y + 3, 4), mod(y + 2, 4)
    mine, other = zl * 4, (1 - zl) * 4
    lo, hi = pl.ds(0, 64), pl.ds(64, 64)

    def copy(c, n):
        if n == FAR:
            return to_y(py.at[c, y_far], far.at[c, 0], c, n, down)
        if n == FAR + 1:
            return to_y(py.at[c, 4 + y_far], far.at[c, 1], c, n, up)
        if n == NEAR:
            return to_y(py.at[c, y_down], near.at[c, 0], c, n, down)
        if n == NEAR + 1:
            return to_y(py.at[c, 4 + y_down], near.at[c, 1], c, n, down)
        if n == NEAR + 2:
            return to_y(py.at[c, y_up], near.at[c, 2], c, n, up)
        if n == NEAR + 3:
            return to_y(py.at[c, 4 + y_up], near.at[c, 3], c, n, up)
        if n == ZSUM:
            return to_y(py.at[c, other + y], zsum.at[c], c, n, zmate)
        if n == ZPRE:
            return to_y(pz.at[c, pl.ds(other, 4)], zpre.at[c], c, n, zmate)
        if n == ZFAR:
            return to_y(pz.at[c, mine + y_far, lo], zfar.at[c, 0], c, n, down)
        if n == ZFAR + 1:
            return to_y(pz.at[c, mine + y_far, hi], zfar.at[c, 1], c, n, up)
        if n == ZNEAR:
            return to_y(pz.at[c, mine + y_down, lo], znear.at[c, 0], c, n, down)
        if n == ZNEAR + 1:
            return to_y(pz.at[c, mine + y_down, hi], znear.at[c, 1], c, n, down)
        if n == ZNEAR + 2:
            return to_y(pz.at[c, mine + y_up, lo], znear.at[c, 2], c, n, up)
        return to_y(pz.at[c, mine + y_up, hi], znear.at[c, 3], c, n, up)

    def added(*parts):
        total = parts[0].astype(F32)
        for part in parts[1:]:
            total = total + part.astype(F32)
        return total.astype(BF)

    def stage_0(c):
        for n in (FAR, FAR + 1, ZPRE, NEAR + 1, NEAR + 2):
            copy(c, n).start()

    def stage_1(c):
        copy(c, FAR).wait_recv()
        py[c, y_down] = added(py[c, y_down], far[c, 0])
        copy(c, FAR + 1).wait_recv()
        py[c, 4 + y_up] = added(py[c, 4 + y_up], far[c, 1])
        copy(c, NEAR).start()
        copy(c, NEAR + 3).start()
        copy(c, ZPRE).wait_recv()
        for d in (2, 1, 3, 0):
            to = mod(y + d, 4)
            pz[c, mine + to] = added(pz[c, mine + to], zpre[c, to])
        for n in (ZFAR, ZFAR + 1, ZNEAR + 1, ZNEAR + 2):
            copy(c, n).start()

    def stage_2(c):
        copy(c, ZFAR).wait_recv()
        copy(c, ZFAR + 1).wait_recv()
        pz[c, mine + y_down, :64] = added(pz[c, mine + y_down, :64], zfar[c, 0])
        pz[c, mine + y_up, 64:] = added(pz[c, mine + y_up, 64:], zfar[c, 1])
        copy(c, ZNEAR).start()
        copy(c, ZNEAR + 3).start()
        for n in range(4):
            copy(c, NEAR + n).wait_recv()
        there = 1 - zl
        py[c, other + y] = added(py[c, other + y], near[c, there], near[c, 2 + there])
        copy(c, ZSUM).start()

    def stage_3(c):
        rows = pl.ds(pl.multiple_of(c * CHUNK, CHUNK), CHUNK)
        for n in range(4):
            copy(c, ZNEAR + n).wait_recv()
        first = pl.ds(pl.multiple_of(c * CHUNK, 64), 64)
        second = pl.ds(pl.multiple_of(c * CHUNK + 64, 64), 64)
        out[first, :ZCOLS] = added(pz[c, mine + y, :64], znear[c, 0], znear[c, 2])
        out[second, :ZCOLS] = added(pz[c, mine + y, 64:], znear[c, 1], znear[c, 3])
        copy(c, ZSUM).wait_recv()
        out[rows, ZCOLS:] = added(py[c, mine + y], near[c, zl], near[c, 2 + zl], zsum[c])

    def step(t, _):
        c = div(t, 4)
        s = mod(t, 4)
        for at, gather in enumerate((gather_0, gather_1, gather_2, gather_3)):
            pl.when(t == at)(gather)
        pl.when(s == 0)(start_chunk)
        attend(c, s)

        @pl.when((t >= 4) & (s == 0))
        def _():
            stage_1(c - 1)

        @pl.when((t >= 4) & (s == 2))
        def _():
            stage_2(c - 1)

        @pl.when((t >= 8) & (s == 0))
        def _():
            stage_3(c - 2)

        @pl.when(s == 3)
        def _():
            pl.when(t == 3)(w_copy.wait)
            project(c)
            stage_0(c)

        return 0

    lax.fori_loop(0, 4 * CHUNKS, step, 0)
    last = CHUNKS - 1
    stage_1(last)
    stage_3(last - 1)
    stage_2(last)
    stage_3(last)

    for n in range(len(kv_sends)):
        pltpu.make_async_remote_copy(
            src_ref=k, dst_ref=kv.at[blk, 0], send_sem=kv_send.at[n],
            recv_sem=kv_recv.at[blk, 0], device_id=(mate, head), device_id_type=MESH,
        ).wait_send()

    def sent(c, _):
        for n in range(14):
            copy(c, n).wait_send()
        return 0

    lax.fori_loop(0, CHUNKS, sent, 0)


def per_device(queries, keys, values, w_out, order):
    vmem = pl.BlockSpec(memory_space=pltpu.VMEM)
    return pl.pallas_call(
        kernel,
        out_shape=jax.ShapeDtypeStruct((CHUNK * CHUNKS, 1024), BF),
        in_specs=[pl.BlockSpec(memory_space=pltpu.SMEM), vmem, vmem, vmem,
                  pl.BlockSpec(memory_space=pl.ANY)],
        out_specs=vmem,
        scratch_shapes=[
            pltpu.VMEM((16, 2, 512, HD), BF),
            pltpu.VMEM((1024, 8192), BF),
            pltpu.VMEM((128, 128), BF),
            pltpu.VMEM((3, 128, 128), BF),
            pltpu.VMEM((SUBS, 256, 1), F32),
            pltpu.VMEM((SUBS, 256, 256), F32),
            pltpu.VMEM((CHUNK, 1024), BF),
            pltpu.VMEM((CHUNKS, 8, CHUNK, YCOLS), BF),
            pltpu.VMEM((CHUNKS, 8, CHUNK, ZCOLS), BF),
            pltpu.VMEM((CHUNKS, 2, CHUNK, YCOLS), BF),
            pltpu.VMEM((CHUNKS, 4, CHUNK, YCOLS), BF),
            pltpu.VMEM((CHUNKS, CHUNK, YCOLS), BF),
            pltpu.VMEM((CHUNKS, 4, CHUNK, ZCOLS), BF),
            pltpu.VMEM((CHUNKS, 2, 64, ZCOLS), BF),
            pltpu.VMEM((CHUNKS, 4, 64, ZCOLS), BF),
            pltpu.SemaphoreType.DMA((30,)),
            pltpu.SemaphoreType.DMA((16, 2)),
            pltpu.SemaphoreType.DMA((CHUNKS, 14)),
            pltpu.SemaphoreType.DMA((CHUNKS, 14)),
            pltpu.SemaphoreType.DMA,
        ],
        compiler_params=pltpu.CompilerParams(
            collective_id=0, has_side_effects=True, vmem_limit_bytes=66_000_000
        ),
        name="prefill",
    )(order, queries, keys, values, w_out)


def solution(mesh):
    placed = (P("blk", "head"), P("blk", "head"), P("blk", "head"), P("head", None), P())
    return jax.shard_map(
        per_device, mesh=mesh, in_specs=placed, out_specs=P("blk", "head"), check_vma=False
    )
```

```python
import jax
import jax.numpy as jnp
from jax import lax
from jax.experimental import pallas as pl
from jax.experimental.pallas import tpu as pltpu
from jax.sharding import PartitionSpec as P

HD = 128
CHUNK = 128
CHUNKS = 4
HEADS = 8
SUBS = 4
ZCOLS = 384
YCOLS = 640
SCALE2 = HD**-0.5 * 1.4426950408889634
HIDDEN = -1e30
MESH = pl.DeviceIdType.MESH
BF = jnp.bfloat16
F32 = jnp.float32
FAR, NEAR, ZSUM, ZPRE, ZFAR, ZNEAR = 0, 2, 6, 7, 8, 10


def mod(a, n):
    return lax.rem(a, n)


def div(a, n):
    return lax.div(a, n)


def kernel(
    order, q, k, v, w_hbm, out,
    kv, w, eye, masks, top, acc, att,
    py, pz, far, near, zsum, zpre, zfar, znear,
    kv_send, kv_recv, send, recv, w_sem,
):
    blk = lax.axis_index("blk")
    head = lax.axis_index("head")
    core = mod(blk, 2)
    x = mod(div(blk, 2), 4)
    zh = div(blk, 8)
    y = div(head, 2)
    zl = mod(head, 2)

    def block(dz, dx):
        return (mod(zh + dz, 2) * 4 + mod(x + dx, 4)) * 2 + core

    left, right, across = block(0, 3), block(0, 1), block(1, 0)
    mate = blk + 1 - 2 * core
    up = mod(y + 1, 4) * 2 + zl
    down = mod(y + 3, 4) * 2 + zl
    zmate = head + 1 - 2 * zl

    barrier = pltpu.get_barrier_semaphore()
    for peer in (left, right, across, mate):
        pl.semaphore_signal(barrier, inc=1, device_id=(peer, head), device_id_type=MESH)
    for peer in (up, down, zmate):
        pl.semaphore_signal(barrier, inc=1, device_id=(blk, peer), device_id_type=MESH)
    pl.semaphore_wait(barrier, 7)

    w_copy = pltpu.make_async_copy(w_hbm, w, w_sem)

    kv_sends = []

    def pass_on(source, part, to, own=False):
        ref = (k, v)[part] if own else kv.at[source, part]
        copy = pltpu.make_async_remote_copy(
            src_ref=ref, dst_ref=kv.at[source, part],
            send_sem=kv_send.at[len(kv_sends)], recv_sem=kv_recv.at[source, part],
            device_id=(to, head), device_id_type=MESH,
        )
        kv_sends.append(0)
        copy.start()

    def arrived(source, part):
        pltpu.make_async_remote_copy(
            src_ref=kv.at[source, part], dst_ref=kv.at[source, part],
            send_sem=kv_send.at[0], recv_sem=kv_recv.at[source, part],
            device_id=(mate, head), device_id_type=MESH,
        ).wait_recv()

    def mate_has(dz, dx):
        source = block(dz, dx) + 1 - 2 * core
        arrived(source, 0)
        arrived(source, 1)

    for to in (across, right, left, mate):
        for part in (0, 1):
            pass_on(blk, part, to, own=True)
    w_copy.start()

    kv[blk, 0] = k[...]
    kv[blk, 1] = v[...]
    row = lax.broadcasted_iota(jnp.int32, (128, 128), 0)
    col = lax.broadcasted_iota(jnp.int32, (128, 128), 1)
    eye[...] = jnp.where(row == col, 1.0, 0.0).astype(BF)
    masks[0] = jnp.zeros((128, 128), BF)
    masks[1] = jnp.where(row > col, HIDDEN, 0.0).astype(BF)
    masks[2] = jnp.full((128, 128), HIDDEN, BF)

    def gather_a0():
        arrived(left, 0)
        pass_on(left, 0, right)
        arrived(across, 0)
        pass_on(across, 0, right)
        pass_on(across, 0, left)

    def gather_a2():
        arrived(right, 1)
        pass_on(right, 1, left)
        arrived(across, 1)
        pass_on(across, 1, right)
        pass_on(across, 1, left)
        arrived(right, 0)
        arrived(left, 1)
        for source in (right, left, across):
            for part in (0, 1):
                pass_on(source, part, mate)

    def gather_1():
        mate_has(0, 1)

    def gather_2():
        two, zleft = block(0, 2), block(1, 3)
        for part in (0, 1):
            arrived(two, part)
            pass_on(two, part, mate)
        arrived(zleft, 0)
        pass_on(zleft, 0, right)
        mate_has(0, 3)

    def gather_3():
        mate_has(0, 2)

    def gather_4():
        zleft, zright = block(1, 3), block(1, 1)
        arrived(zright, 1)
        pass_on(zright, 1, left)
        arrived(zleft, 1)
        arrived(zright, 0)
        for source in (zright, zleft):
            for part in (0, 1):
                pass_on(source, part, mate)
        mate_has(1, 0)

    def gather_5():
        mate_has(1, 1)

    def gather_6():
        ztwo = block(1, 2)
        for part in (0, 1):
            arrived(ztwo, part)
            pass_on(ztwo, part, mate)
        mate_has(1, 3)

    def gather_7():
        mate_has(1, 2)

    def attend(c, places, first=False):
        rows = pl.ds(pl.multiple_of(c * CHUNK, CHUNK), CHUNK)
        query_pos = 2 * order[2 * blk + div(c, 2)] + mod(c, 2)
        chips = [mod(zh + dz, 2) * 4 + mod(x + dx, 4) for dz, dx in places]
        key_rows, value_rows = [], []
        ones = jnp.ones((128, 128), BF)
        for chip in chips:
            for b in (2 * chip, 2 * chip + 1):
                for t in range(4):
                    key_pos = 2 * order[2 * b + t // 2] + t % 2
                    kind = (key_pos > query_pos).astype(jnp.int32) + (
                        key_pos >= query_pos
                    ).astype(jnp.int32)
                    part = slice(t * 128, (t + 1) * 128)
                    key_rows.append(jnp.concatenate([kv[b, 0, part, :], masks[kind]], axis=1))
                    value_rows.append(jnp.concatenate([kv[b, 1, part, :], ones], axis=1))
        key_tile = jnp.concatenate(key_rows, axis=0)
        value_tile = jnp.concatenate(value_rows, axis=0)
        for u in range(SUBS):
            q_rows = [
                jnp.concatenate([q[rows, h * HD : (h + 1) * HD], eye[...]], axis=1)
                for h in (2 * u, 2 * u + 1)
            ]
            score = lax.dot_general(
                jnp.concatenate(q_rows, axis=0), key_tile,
                (((1,), (1,)), ((), ())), preferred_element_type=F32,
            )
            new = jnp.max(score, axis=1, keepdims=True) * SCALE2
            if not first:
                old = top[c, u]
                new = jnp.maximum(old, new)
            weight = jnp.exp2(score * SCALE2 - new).astype(BF)
            part = jnp.dot(weight, value_tile, preferred_element_type=F32)
            acc[c, u] = part if first else acc[c, u] * jnp.exp2(old - new) + part
            top[c, u] = new

    def project(c):
        for u in range(SUBS):
            mean = (acc[c, u, :, :HD] / acc[c, u, :, HD:]).astype(BF)
            for h in range(2):
                at = (2 * u + h) * HD
                att[:, at : at + HD] = mean[h * CHUNK : (h + 1) * CHUNK]

        def one(i, _):
            to_y = mod(y + 2 + div(i, 2), 4)
            to_z = mod(i, 2)
            columns = pl.ds(pl.multiple_of((to_y * 2 + to_z) * 1024, 1024), 1024)
            part = jnp.dot(att[...], w[:, columns], preferred_element_type=F32).astype(BF)
            pz[c, to_z * 4 + to_y] = part[:, :ZCOLS]
            py[c, to_z * 4 + to_y] = part[:, ZCOLS:]
            return 0

        lax.fori_loop(0, 8, one, 0)

    def to_y(src, dst, c, n, peer):
        return pltpu.make_async_remote_copy(
            src_ref=src, dst_ref=dst, send_sem=send.at[c, n], recv_sem=recv.at[c, n],
            device_id=(blk, peer), device_id_type=MESH,
        )

    y_up, y_down, y_far = mod(y + 1, 4), mod(y + 3, 4), mod(y + 2, 4)
    mine, other = zl * 4, (1 - zl) * 4
    lo, hi = pl.ds(0, 64), pl.ds(64, 64)

    def copy(c, n):
        if n == FAR:
            return to_y(py.at[c, y_far], far.at[c, 0], c, n, down)
        if n == FAR + 1:
            return to_y(py.at[c, 4 + y_far], far.at[c, 1], c, n, up)
        if n == NEAR:
            return to_y(py.at[c, y_down], near.at[c, 0], c, n, down)
        if n == NEAR + 1:
            return to_y(py.at[c, 4 + y_down], near.at[c, 1], c, n, down)
        if n == NEAR + 2:
            return to_y(py.at[c, y_up], near.at[c, 2], c, n, up)
        if n == NEAR + 3:
            return to_y(py.at[c, 4 + y_up], near.at[c, 3], c, n, up)
        if n == ZSUM:
            return to_y(py.at[c, other + y], zsum.at[c], c, n, zmate)
        if n == ZPRE:
            return to_y(pz.at[c, pl.ds(other, 4)], zpre.at[c], c, n, zmate)
        if n == ZFAR:
            return to_y(pz.at[c, mine + y_far, lo], zfar.at[c, 0], c, n, down)
        if n == ZFAR + 1:
            return to_y(pz.at[c, mine + y_far, hi], zfar.at[c, 1], c, n, up)
        if n == ZNEAR:
            return to_y(pz.at[c, mine + y_down, lo], znear.at[c, 0], c, n, down)
        if n == ZNEAR + 1:
            return to_y(pz.at[c, mine + y_down, hi], znear.at[c, 1], c, n, down)
        if n == ZNEAR + 2:
            return to_y(pz.at[c, mine + y_up, lo], znear.at[c, 2], c, n, up)
        return to_y(pz.at[c, mine + y_up, hi], znear.at[c, 3], c, n, up)

    def added(*parts):
        total = parts[0].astype(F32)
        for part in parts[1:]:
            total = total + part.astype(F32)
        return total.astype(BF)

    def stage_0(c):
        for n in (FAR, FAR + 1, ZPRE, NEAR + 1, NEAR + 2):
            copy(c, n).start()

    def stage_1(c):
        copy(c, FAR).wait_recv()
        py[c, y_down] = added(py[c, y_down], far[c, 0])
        copy(c, FAR + 1).wait_recv()
        py[c, 4 + y_up] = added(py[c, 4 + y_up], far[c, 1])
        copy(c, NEAR).start()
        copy(c, NEAR + 3).start()

    def stage_1b(c):
        copy(c, ZPRE).wait_recv()
        for d in (2, 1, 3, 0):
            to = mod(y + d, 4)
            pz[c, mine + to] = added(pz[c, mine + to], zpre[c, to])
        for n in (ZFAR, ZFAR + 1, ZNEAR + 1, ZNEAR + 2):
            copy(c, n).start()

    def stage_2(c):
        for n in range(4):
            copy(c, NEAR + n).wait_recv()
        there = 1 - zl
        py[c, other + y] = added(py[c, other + y], near[c, there], near[c, 2 + there])
        copy(c, ZSUM).start()
        copy(c, ZFAR).wait_recv()
        copy(c, ZFAR + 1).wait_recv()
        pz[c, mine + y_down, :64] = added(pz[c, mine + y_down, :64], zfar[c, 0])
        pz[c, mine + y_up, 64:] = added(pz[c, mine + y_up, 64:], zfar[c, 1])
        copy(c, ZNEAR).start()
        copy(c, ZNEAR + 3).start()

    def stage_3(c):
        rows = pl.ds(pl.multiple_of(c * CHUNK, CHUNK), CHUNK)
        for n in range(4):
            copy(c, ZNEAR + n).wait_recv()
        first = pl.ds(pl.multiple_of(c * CHUNK, 64), 64)
        second = pl.ds(pl.multiple_of(c * CHUNK + 64, 64), 64)
        out[first, :ZCOLS] = added(pz[c, mine + y, :64], znear[c, 0], znear[c, 2])
        out[second, :ZCOLS] = added(pz[c, mine + y, 64:], znear[c, 1], znear[c, 3])
        copy(c, ZSUM).wait_recv()
        out[rows, ZCOLS:] = added(py[c, mine + y], near[c, zl], near[c, 2 + zl], zsum[c])

    def early(c, _):
        attend(c, ((0, 0),), first=True)
        pl.when(c == 1)(gather_a0)
        pl.when(c == 2)(gather_a2)
        return 0

    waits = (gather_1, gather_2, gather_3, gather_4, gather_5, gather_6, gather_7)

    def one_chip(n, _):
        for at, gather in enumerate(waits):
            pl.when(n == at + 1)(gather)
        m = mod(n, 4)
        attend(0, ((div(n, 4), m + div(m, 2) - 2 * div(m, 3)),))
        return 0

    def step(n, _):
        c = div(n, 3)
        s = mod(n, 3)
        attend(c, ((div(s + 1, 2), mod(s + 1, 2)), (div(s, 2), 3 - mod(s, 2))))

        @pl.when(s == 1)
        def _():
            stage_1(c - 1)
            pl.when(c >= 2)(lambda: stage_3(c - 2))

        @pl.when(s == 2)
        def _():
            stage_1b(c - 1)
            attend(c, ((1, 2),))
            project(c)
            stage_2(c - 1)
            stage_0(c)

        return 0

    mate_has(0, 0)
    lax.fori_loop(0, CHUNKS, early, 0)
    lax.fori_loop(1, 8, one_chip, 0)
    w_copy.wait()
    project(0)
    stage_0(0)
    lax.fori_loop(3, 3 * CHUNKS, step, 0)
    last = CHUNKS - 1
    stage_1(last)
    stage_3(last - 1)
    stage_1b(last)
    stage_2(last)
    stage_3(last)

    for n in range(len(kv_sends)):
        pltpu.make_async_remote_copy(
            src_ref=k, dst_ref=kv.at[blk, 0], send_sem=kv_send.at[n],
            recv_sem=kv_recv.at[blk, 0], device_id=(mate, head), device_id_type=MESH,
        ).wait_send()

    def sent(c, _):
        for n in range(14):
            copy(c, n).wait_send()
        return 0

    lax.fori_loop(0, CHUNKS, sent, 0)


def per_device(queries, keys, values, w_out, order):
    vmem = pl.BlockSpec(memory_space=pltpu.VMEM)
    return pl.pallas_call(
        kernel,
        out_shape=jax.ShapeDtypeStruct((CHUNK * CHUNKS, 1024), BF),
        in_specs=[pl.BlockSpec(memory_space=pltpu.SMEM), vmem, vmem, vmem,
                  pl.BlockSpec(memory_space=pl.ANY)],
        out_specs=vmem,
        scratch_shapes=[
            pltpu.VMEM((16, 2, 512, HD), BF),
            pltpu.VMEM((1024, 8192), BF),
            pltpu.VMEM((128, 128), BF),
            pltpu.VMEM((3, 128, 128), BF),
            pltpu.VMEM((CHUNKS, SUBS, 256, 1), F32),
            pltpu.VMEM((CHUNKS, SUBS, 256, 256), F32),
            pltpu.VMEM((CHUNK, 1024), BF),
            pltpu.VMEM((CHUNKS, 8, CHUNK, YCOLS), BF),
            pltpu.VMEM((CHUNKS, 8, CHUNK, ZCOLS), BF),
            pltpu.VMEM((CHUNKS, 2, CHUNK, YCOLS), BF),
            pltpu.VMEM((CHUNKS, 4, CHUNK, YCOLS), BF),
            pltpu.VMEM((CHUNKS, CHUNK, YCOLS), BF),
            pltpu.VMEM((CHUNKS, 4, CHUNK, ZCOLS), BF),
            pltpu.VMEM((CHUNKS, 2, 64, ZCOLS), BF),
            pltpu.VMEM((CHUNKS, 4, 64, ZCOLS), BF),
            pltpu.SemaphoreType.DMA((30,)),
            pltpu.SemaphoreType.DMA((16, 2)),
            pltpu.SemaphoreType.DMA((CHUNKS, 14)),
            pltpu.SemaphoreType.DMA((CHUNKS, 14)),
            pltpu.SemaphoreType.DMA,
        ],
        compiler_params=pltpu.CompilerParams(
            collective_id=0, has_side_effects=True, vmem_limit_bytes=66_000_000
        ),
        name="prefill",
    )(order, queries, keys, values, w_out)


def solution(mesh):
    placed = (P("blk", "head"), P("blk", "head"), P("blk", "head"), P("head", None), P())
    return jax.shard_map(
        per_device, mesh=mesh, in_specs=placed, out_specs=P("blk", "head"), check_vma=False
    )
```

```python
import jax
import jax.numpy as jnp
from jax import lax
from jax.experimental import pallas as pl
from jax.experimental.pallas import tpu as pltpu
from jax.sharding import PartitionSpec as P

HD = 128
CHUNK = 128
CHUNKS = 4
HEADS = 8
SUBS = 4
ZCOLS = 384
YCOLS = 640
SCALE2 = HD**-0.5 * 1.4426950408889634
HIDDEN = -1e30
MESH = pl.DeviceIdType.MESH
BF = jnp.bfloat16
F32 = jnp.float32
FAR, NEAR, ZSUM, ZPRE, ZFAR, ZNEAR = 0, 2, 6, 7, 8, 10


def mod(a, n):
    return lax.rem(a, n)


def div(a, n):
    return lax.div(a, n)


def kernel(
    order, q_hbm, k, v, w_hbm, out,
    q, kv, w, eye, masks, top, acc, att,
    py, pz, far, near, zsum, zpre, zfar, znear,
    kv_send, kv_recv, send, recv, w_sem, in_sem,
):
    blk = lax.axis_index("blk")
    head = lax.axis_index("head")
    core = mod(blk, 2)
    x = mod(div(blk, 2), 4)
    zh = div(blk, 8)
    y = div(head, 2)
    zl = mod(head, 2)

    def block(dz, dx):
        return (mod(zh + dz, 2) * 4 + mod(x + dx, 4)) * 2 + core

    left, right, across = block(0, 3), block(0, 1), block(1, 0)
    mate = blk + 1 - 2 * core
    up = mod(y + 1, 4) * 2 + zl
    down = mod(y + 3, 4) * 2 + zl
    zmate = head + 1 - 2 * zl

    loads = [
        pltpu.make_async_copy(src, dst, in_sem.at[n])
        for n, (src, dst) in enumerate(((q_hbm, q), (k, kv.at[blk, 0]), (v, kv.at[blk, 1])))
    ]
    for load in loads:
        load.start()
    barrier = pltpu.get_barrier_semaphore()
    for peer in (left, right, across, mate):
        pl.semaphore_signal(barrier, inc=1, device_id=(peer, head), device_id_type=MESH)
    for peer in (up, down, zmate):
        pl.semaphore_signal(barrier, inc=1, device_id=(blk, peer), device_id_type=MESH)
    pl.semaphore_wait(barrier, 7)

    w_copy = pltpu.make_async_copy(w_hbm, w, w_sem)

    kv_sends = []

    def pass_on(source, part, to, own=False):
        ref = (k, v)[part] if own else kv.at[source, part]
        copy = pltpu.make_async_remote_copy(
            src_ref=ref, dst_ref=kv.at[source, part],
            send_sem=kv_send.at[len(kv_sends)], recv_sem=kv_recv.at[source, part],
            device_id=(to, head), device_id_type=MESH,
        )
        kv_sends.append(0)
        copy.start()

    def arrived(source, part):
        pltpu.make_async_remote_copy(
            src_ref=kv.at[source, part], dst_ref=kv.at[source, part],
            send_sem=kv_send.at[0], recv_sem=kv_recv.at[source, part],
            device_id=(mate, head), device_id_type=MESH,
        ).wait_recv()

    def mate_has(dz, dx):
        source = block(dz, dx) + 1 - 2 * core
        arrived(source, 0)
        arrived(source, 1)

    for to in (across, right, left, mate):
        for part in (0, 1):
            pass_on(blk, part, to, own=True)
    w_copy.start()

    row = lax.broadcasted_iota(jnp.int32, (128, 128), 0)
    col = lax.broadcasted_iota(jnp.int32, (128, 128), 1)
    eye[...] = jnp.where(row == col, 1.0, 0.0).astype(BF)
    masks[0] = jnp.zeros((128, 128), BF)
    masks[1] = jnp.where(row > col, HIDDEN, 0.0).astype(BF)
    masks[2] = jnp.full((128, 128), HIDDEN, BF)

    def gather_a0():
        arrived(left, 0)
        pass_on(left, 0, right)
        arrived(across, 0)
        pass_on(across, 0, right)
        pass_on(across, 0, left)

    def gather_a2():
        arrived(right, 1)
        pass_on(right, 1, left)
        arrived(across, 1)
        pass_on(across, 1, right)
        pass_on(across, 1, left)
        arrived(right, 0)
        arrived(left, 1)
        for source in (right, left, across):
            for part in (0, 1):
                pass_on(source, part, mate)

    def gather_1():
        mate_has(0, 1)

    def gather_2():
        two, zleft = block(0, 2), block(1, 3)
        for part in (0, 1):
            arrived(two, part)
            pass_on(two, part, mate)
        arrived(zleft, 0)
        pass_on(zleft, 0, right)
        mate_has(0, 3)

    def gather_3():
        mate_has(0, 2)

    def gather_4():
        zleft, zright = block(1, 3), block(1, 1)
        arrived(zright, 1)
        pass_on(zright, 1, left)
        arrived(zleft, 1)
        arrived(zright, 0)
        for source in (zright, zleft):
            for part in (0, 1):
                pass_on(source, part, mate)
        mate_has(1, 0)

    def gather_5():
        mate_has(1, 1)

    def gather_6():
        ztwo = block(1, 2)
        for part in (0, 1):
            arrived(ztwo, part)
            pass_on(ztwo, part, mate)
        mate_has(1, 3)

    def gather_7():
        mate_has(1, 2)

    def attend(c, places, first=False):
        rows = pl.ds(pl.multiple_of(c * CHUNK, CHUNK), CHUNK)
        query_pos = 2 * order[2 * blk + div(c, 2)] + mod(c, 2)
        chips = [mod(zh + dz, 2) * 4 + mod(x + dx, 4) for dz, dx in places]
        key_rows, value_rows = [], []
        ones = jnp.ones((128, 128), BF)
        for chip in chips:
            for b in (2 * chip, 2 * chip + 1):
                for t in range(4):
                    key_pos = 2 * order[2 * b + t // 2] + t % 2
                    kind = (key_pos > query_pos).astype(jnp.int32) + (
                        key_pos >= query_pos
                    ).astype(jnp.int32)
                    part = slice(t * 128, (t + 1) * 128)
                    key_rows.append(jnp.concatenate([kv[b, 0, part, :], masks[kind]], axis=1))
                    value_rows.append(jnp.concatenate([kv[b, 1, part, :], ones], axis=1))
        key_tile = jnp.concatenate(key_rows, axis=0)
        value_tile = jnp.concatenate(value_rows, axis=0)
        for u in range(SUBS):
            q_rows = [
                jnp.concatenate([q[rows, h * HD : (h + 1) * HD], eye[...]], axis=1)
                for h in (2 * u, 2 * u + 1)
            ]
            score = lax.dot_general(
                jnp.concatenate(q_rows, axis=0), key_tile,
                (((1,), (1,)), ((), ())), preferred_element_type=F32,
            )
            new = jnp.max(score, axis=1, keepdims=True) * SCALE2
            if not first:
                old = top[c, u]
                new = jnp.maximum(old, new)
            weight = jnp.exp2(score * SCALE2 - new).astype(BF)
            part = jnp.dot(weight, value_tile, preferred_element_type=F32)
            acc[c, u] = part if first else acc[c, u] * jnp.exp2(old - new) + part
            top[c, u] = new

    def project(c):
        for u in range(SUBS):
            mean = (acc[c, u, :, :HD] / acc[c, u, :, HD:]).astype(BF)
            for h in range(2):
                at = (2 * u + h) * HD
                att[:, at : at + HD] = mean[h * CHUNK : (h + 1) * CHUNK]

        def one(i, _):
            to = mod(y + 2 + i, 4)
            columns = pl.ds(pl.multiple_of(to * 2048, 2048), 2048)
            part = jnp.dot(att[...], w[:, columns], preferred_element_type=F32).astype(BF)
            for z in range(2):
                pz[c, z * 4 + to] = part[:, z * 1024 : z * 1024 + ZCOLS]
                py[c, z * 4 + to] = part[:, z * 1024 + ZCOLS : (z + 1) * 1024]
            return 0

        lax.fori_loop(0, 4, one, 0)

    def to_y(src, dst, c, n, peer):
        return pltpu.make_async_remote_copy(
            src_ref=src, dst_ref=dst, send_sem=send.at[c, n], recv_sem=recv.at[c, n],
            device_id=(blk, peer), device_id_type=MESH,
        )

    y_up, y_down, y_far = mod(y + 1, 4), mod(y + 3, 4), mod(y + 2, 4)
    mine, other = zl * 4, (1 - zl) * 4
    lo, hi = pl.ds(0, 64), pl.ds(64, 64)

    def copy(c, n):
        if n == FAR:
            return to_y(py.at[c, y_far], far.at[c, 0], c, n, down)
        if n == FAR + 1:
            return to_y(py.at[c, 4 + y_far], far.at[c, 1], c, n, up)
        if n == NEAR:
            return to_y(py.at[c, y_down], near.at[c, 0], c, n, down)
        if n == NEAR + 1:
            return to_y(py.at[c, 4 + y_down], near.at[c, 1], c, n, down)
        if n == NEAR + 2:
            return to_y(py.at[c, y_up], near.at[c, 2], c, n, up)
        if n == NEAR + 3:
            return to_y(py.at[c, 4 + y_up], near.at[c, 3], c, n, up)
        if n == ZSUM:
            return to_y(py.at[c, other + y], zsum.at[c], c, n, zmate)
        if n == ZPRE:
            return to_y(pz.at[c, pl.ds(other, 4)], zpre.at[c], c, n, zmate)
        if n == ZFAR:
            return to_y(pz.at[c, mine + y_far, lo], zfar.at[c, 0], c, n, down)
        if n == ZFAR + 1:
            return to_y(pz.at[c, mine + y_far, hi], zfar.at[c, 1], c, n, up)
        if n == ZNEAR:
            return to_y(pz.at[c, mine + y_down, lo], znear.at[c, 0], c, n, down)
        if n == ZNEAR + 1:
            return to_y(pz.at[c, mine + y_down, hi], znear.at[c, 1], c, n, down)
        if n == ZNEAR + 2:
            return to_y(pz.at[c, mine + y_up, lo], znear.at[c, 2], c, n, up)
        return to_y(pz.at[c, mine + y_up, hi], znear.at[c, 3], c, n, up)

    def added(*parts):
        total = parts[0].astype(F32)
        for part in parts[1:]:
            total = total + part.astype(F32)
        return total.astype(BF)

    def stage_0(c):
        for n in (ZPRE, FAR, FAR + 1, NEAR + 1, NEAR + 2):
            copy(c, n).start()

    def stage_1(c):
        copy(c, FAR).wait_recv()
        py[c, y_down] = added(py[c, y_down], far[c, 0])
        copy(c, FAR + 1).wait_recv()
        py[c, 4 + y_up] = added(py[c, 4 + y_up], far[c, 1])
        copy(c, NEAR).start()
        copy(c, NEAR + 3).start()

    def stage_1b(c):
        copy(c, ZPRE).wait_recv()
        for d in (2, 1, 3, 0):
            to = mod(y + d, 4)
            pz[c, mine + to] = added(pz[c, mine + to], zpre[c, to])
        for n in (ZFAR, ZFAR + 1, ZNEAR + 1, ZNEAR + 2):
            copy(c, n).start()

    def stage_2(c):
        for n in range(4):
            copy(c, NEAR + n).wait_recv()
        there = 1 - zl
        py[c, other + y] = added(py[c, other + y], near[c, there], near[c, 2 + there])
        copy(c, ZSUM).start()
        copy(c, ZFAR).wait_recv()
        copy(c, ZFAR + 1).wait_recv()
        pz[c, mine + y_down, :64] = added(pz[c, mine + y_down, :64], zfar[c, 0])
        pz[c, mine + y_up, 64:] = added(pz[c, mine + y_up, 64:], zfar[c, 1])
        copy(c, ZNEAR).start()
        copy(c, ZNEAR + 3).start()

    def stage_3(c):
        rows = pl.ds(pl.multiple_of(c * CHUNK, CHUNK), CHUNK)
        for n in range(4):
            copy(c, ZNEAR + n).wait_recv()
        first = pl.ds(pl.multiple_of(c * CHUNK, 64), 64)
        second = pl.ds(pl.multiple_of(c * CHUNK + 64, 64), 64)
        out[first, :ZCOLS] = added(pz[c, mine + y, :64], znear[c, 0], znear[c, 2])
        out[second, :ZCOLS] = added(pz[c, mine + y, 64:], znear[c, 1], znear[c, 3])
        copy(c, ZSUM).wait_recv()
        out[rows, ZCOLS:] = added(py[c, mine + y], near[c, zl], near[c, 2 + zl], zsum[c])

    def early(c, _):
        attend(c, ((0, 0),), first=True)
        pl.when(c == 1)(gather_a0)
        pl.when(c == 2)(gather_a2)
        return 0

    waits = (gather_1, gather_2, gather_3, gather_4, gather_5, gather_6, gather_7)

    def one_chip(n, _):
        for at, gather in enumerate(waits):
            pl.when(n == at + 1)(gather)
        m = mod(n, 4)
        attend(0, ((div(n, 4), m + div(m, 2) - 2 * div(m, 3)),))
        return 0

    def step(n, _):
        c = div(n, 3)
        s = mod(n, 3)
        attend(c, ((div(s + 1, 2), mod(s + 1, 2)), (div(s, 2), 3 - mod(s, 2))))

        @pl.when(s == 1)
        def _():
            stage_1(c - 1)

        @pl.when(s == 2)
        def _():
            attend(c, ((1, 2),))
            stage_1b(c - 1)
            project(c)
            stage_0(c)
            stage_2(c - 1)
            pl.when(c >= 2)(lambda: stage_3(c - 2))

        return 0

    for load in loads:
        load.wait()
    mate_has(0, 0)
    lax.fori_loop(0, CHUNKS, early, 0)
    lax.fori_loop(1, 8, one_chip, 0)
    w_copy.wait()
    project(0)
    stage_0(0)
    lax.fori_loop(3, 3 * CHUNKS, step, 0)
    last = CHUNKS - 1
    stage_1(last)
    stage_3(last - 1)
    stage_1b(last)
    stage_2(last)
    stage_3(last)

    for n in range(len(kv_sends)):
        pltpu.make_async_remote_copy(
            src_ref=k, dst_ref=kv.at[blk, 0], send_sem=kv_send.at[n],
            recv_sem=kv_recv.at[blk, 0], device_id=(mate, head), device_id_type=MESH,
        ).wait_send()

    def sent(c, _):
        for n in range(14):
            copy(c, n).wait_send()
        return 0

    lax.fori_loop(0, CHUNKS, sent, 0)


def per_device(queries, keys, values, w_out, order):
    vmem = pl.BlockSpec(memory_space=pltpu.VMEM)
    return pl.pallas_call(
        kernel,
        out_shape=jax.ShapeDtypeStruct((CHUNK * CHUNKS, 1024), BF),
        in_specs=[pl.BlockSpec(memory_space=pltpu.SMEM)] + [pl.BlockSpec(memory_space=pl.ANY)] * 4,
        out_specs=vmem,
        scratch_shapes=[
            pltpu.VMEM((CHUNK * CHUNKS, 1024), BF),
            pltpu.VMEM((16, 2, 512, HD), BF),
            pltpu.VMEM((1024, 8192), BF),
            pltpu.VMEM((128, 128), BF),
            pltpu.VMEM((3, 128, 128), BF),
            pltpu.VMEM((CHUNKS, SUBS, 256, 1), F32),
            pltpu.VMEM((CHUNKS, SUBS, 256, 256), F32),
            pltpu.VMEM((CHUNK, 1024), BF),
            pltpu.VMEM((CHUNKS, 8, CHUNK, YCOLS), BF),
            pltpu.VMEM((CHUNKS, 8, CHUNK, ZCOLS), BF),
            pltpu.VMEM((CHUNKS, 2, CHUNK, YCOLS), BF),
            pltpu.VMEM((CHUNKS, 4, CHUNK, YCOLS), BF),
            pltpu.VMEM((CHUNKS, CHUNK, YCOLS), BF),
            pltpu.VMEM((CHUNKS, 4, CHUNK, ZCOLS), BF),
            pltpu.VMEM((CHUNKS, 2, 64, ZCOLS), BF),
            pltpu.VMEM((CHUNKS, 4, 64, ZCOLS), BF),
            pltpu.SemaphoreType.DMA((30,)),
            pltpu.SemaphoreType.DMA((16, 2)),
            pltpu.SemaphoreType.DMA((CHUNKS, 14)),
            pltpu.SemaphoreType.DMA((CHUNKS, 14)),
            pltpu.SemaphoreType.DMA,
            pltpu.SemaphoreType.DMA((3,)),
        ],
        compiler_params=pltpu.CompilerParams(
            collective_id=0, has_side_effects=True, vmem_limit_bytes=66_000_000
        ),
        name="prefill",
    )(order, queries, keys, values, w_out)


def solution(mesh):
    placed = (P("blk", "head"), P("blk", "head"), P("blk", "head"), P("head", None), P())
    return jax.shard_map(
        per_device, mesh=mesh, in_specs=placed, out_specs=P("blk", "head"), check_vma=False
    )
```

```python
import jax
import jax.numpy as jnp
from jax import lax
from jax.experimental import pallas as pl
from jax.experimental.pallas import tpu as pltpu
from jax.sharding import PartitionSpec as P

HD = 128
CHUNK = 128
CHUNKS = 4
HEADS = 8
SUBS = 4
ZCOLS = 384
YCOLS = 640
SCALE2 = HD**-0.5 * 1.4426950408889634
HIDDEN = -1e30
MESH = pl.DeviceIdType.MESH
BF = jnp.bfloat16
F32 = jnp.float32
FAR, NEAR, ZSUM, ZPRE, ZFAR, ZNEAR = 0, 2, 6, 7, 8, 10


def mod(a, n):
    return lax.rem(a, n)


def div(a, n):
    return lax.div(a, n)


def kernel(
    order, q_hbm, k, v, w_hbm, out,
    q, kv, w, eye, masks, top, acc, att,
    py, pz, far, near, zsum, zpre, zfar, znear,
    kv_send, kv_recv, send, recv, w_sem, in_sem,
):
    blk = lax.axis_index("blk")
    head = lax.axis_index("head")
    core = mod(blk, 2)
    x = mod(div(blk, 2), 4)
    zh = div(blk, 8)
    y = div(head, 2)
    zl = mod(head, 2)

    def block(dz, dx):
        return (mod(zh + dz, 2) * 4 + mod(x + dx, 4)) * 2 + core

    left, right, across = block(0, 3), block(0, 1), block(1, 0)
    mate = blk + 1 - 2 * core
    up = mod(y + 1, 4) * 2 + zl
    down = mod(y + 3, 4) * 2 + zl
    zmate = head + 1 - 2 * zl

    loads = [
        pltpu.make_async_copy(src, dst, in_sem.at[n])
        for n, (src, dst) in enumerate(((q_hbm, q), (k, kv.at[blk, 0]), (v, kv.at[blk, 1])))
    ]
    for load in loads:
        load.start()
    barrier = pltpu.get_barrier_semaphore()
    for peer in (left, right, across, mate):
        pl.semaphore_signal(barrier, inc=1, device_id=(peer, head), device_id_type=MESH)
    for peer in (up, down, zmate):
        pl.semaphore_signal(barrier, inc=1, device_id=(blk, peer), device_id_type=MESH)
    pl.semaphore_wait(barrier, 7)

    w_copy = pltpu.make_async_copy(w_hbm, w, w_sem)

    kv_sends = []

    def pass_on(source, part, to, own=False):
        ref = (k, v)[part] if own else kv.at[source, part]
        copy = pltpu.make_async_remote_copy(
            src_ref=ref, dst_ref=kv.at[source, part],
            send_sem=kv_send.at[len(kv_sends)], recv_sem=kv_recv.at[source, part],
            device_id=(to, head), device_id_type=MESH,
        )
        kv_sends.append(0)
        copy.start()

    def arrived(source, part):
        pltpu.make_async_remote_copy(
            src_ref=kv.at[source, part], dst_ref=kv.at[source, part],
            send_sem=kv_send.at[0], recv_sem=kv_recv.at[source, part],
            device_id=(mate, head), device_id_type=MESH,
        ).wait_recv()

    def mate_has(dz, dx):
        source = block(dz, dx) + 1 - 2 * core
        arrived(source, 0)
        arrived(source, 1)

    for to in (across, right, left, mate):
        for part in (0, 1):
            pass_on(blk, part, to, own=True)
    w_copy.start()

    row = lax.broadcasted_iota(jnp.int32, (128, 128), 0)
    col = lax.broadcasted_iota(jnp.int32, (128, 128), 1)
    eye[...] = jnp.where(row == col, 1.0, 0.0).astype(BF)
    masks[0] = jnp.zeros((128, 128), BF)
    masks[1] = jnp.where(row > col, HIDDEN, 0.0).astype(BF)
    masks[2] = jnp.full((128, 128), HIDDEN, BF)

    def gather_a0():
        arrived(left, 0)
        pass_on(left, 0, right)
        arrived(across, 0)
        pass_on(across, 0, right)
        pass_on(across, 0, left)

    def gather_a2():
        arrived(right, 1)
        pass_on(right, 1, left)
        arrived(across, 1)
        pass_on(across, 1, right)
        pass_on(across, 1, left)
        arrived(right, 0)
        arrived(left, 1)
        for source in (right, left, across):
            for part in (0, 1):
                pass_on(source, part, mate)

    def gather_1():
        mate_has(0, 1)

    def gather_2():
        two, zleft = block(0, 2), block(1, 3)
        for part in (0, 1):
            arrived(two, part)
            pass_on(two, part, mate)
        arrived(zleft, 0)
        pass_on(zleft, 0, right)
        mate_has(0, 3)

    def gather_3():
        mate_has(0, 2)

    def gather_4():
        zleft, zright = block(1, 3), block(1, 1)
        arrived(zright, 1)
        pass_on(zright, 1, left)
        arrived(zleft, 1)
        arrived(zright, 0)
        for source in (zright, zleft):
            for part in (0, 1):
                pass_on(source, part, mate)
        mate_has(1, 0)

    def gather_5():
        mate_has(1, 1)

    def gather_6():
        ztwo = block(1, 2)
        for part in (0, 1):
            arrived(ztwo, part)
            pass_on(ztwo, part, mate)
        mate_has(1, 3)

    def gather_7():
        mate_has(1, 2)

    def attend(c, places, first=False):
        rows = pl.ds(pl.multiple_of(c * CHUNK, CHUNK), CHUNK)
        query_pos = 2 * order[2 * blk + div(c, 2)] + mod(c, 2)
        chips = [mod(zh + dz, 2) * 4 + mod(x + dx, 4) for dz, dx in places]
        key_rows, value_rows = [], []
        ones = jnp.ones((128, 128), BF)
        for chip in chips:
            for b in (2 * chip, 2 * chip + 1):
                for t in range(4):
                    key_pos = 2 * order[2 * b + t // 2] + t % 2
                    kind = (key_pos > query_pos).astype(jnp.int32) + (
                        key_pos >= query_pos
                    ).astype(jnp.int32)
                    part = slice(t * 128, (t + 1) * 128)
                    key_rows.append(jnp.concatenate([kv[b, 0, part, :], masks[kind]], axis=1))
                    value_rows.append(jnp.concatenate([kv[b, 1, part, :], ones], axis=1))
        key_tile = jnp.concatenate(key_rows, axis=0)
        value_tile = jnp.concatenate(value_rows, axis=0)
        scores = []
        for u in range(SUBS):
            q_rows = [
                jnp.concatenate([q[rows, h * HD : (h + 1) * HD], eye[...]], axis=1)
                for h in (2 * u, 2 * u + 1)
            ]
            scores.append(lax.dot_general(
                jnp.concatenate(q_rows, axis=0), key_tile,
                (((1,), (1,)), ((), ())), preferred_element_type=F32,
            ))
        weights = []
        for u, score in enumerate(scores):
            new = jnp.max(score, axis=1, keepdims=True) * SCALE2
            fade = None
            if not first:
                old = top[c, u]
                new = jnp.maximum(old, new)
                fade = jnp.exp2(old - new)
            top[c, u] = new
            weights.append((jnp.exp2(score * SCALE2 - new).astype(BF), fade))
        for u, (weight, fade) in enumerate(weights):
            part = jnp.dot(weight, value_tile, preferred_element_type=F32)
            acc[c, u] = part if first else acc[c, u] * fade + part

    def project(c):
        for u in range(SUBS):
            mean = (acc[c, u, :, :HD] / acc[c, u, :, HD:]).astype(BF)
            for h in range(2):
                at = (2 * u + h) * HD
                att[:, at : at + HD] = mean[h * CHUNK : (h + 1) * CHUNK]

        def one(i, _):
            to = mod(y + 2 + i, 4)
            columns = pl.ds(pl.multiple_of(to * 2048, 2048), 2048)
            part = jnp.dot(att[...], w[:, columns], preferred_element_type=F32).astype(BF)
            for z in range(2):
                pz[c, z * 4 + to] = part[:, z * 1024 : z * 1024 + ZCOLS]
                py[c, z * 4 + to] = part[:, z * 1024 + ZCOLS : (z + 1) * 1024]
            return 0

        lax.fori_loop(0, 4, one, 0)

    def to_y(src, dst, c, n, peer):
        return pltpu.make_async_remote_copy(
            src_ref=src, dst_ref=dst, send_sem=send.at[c, n], recv_sem=recv.at[c, n],
            device_id=(blk, peer), device_id_type=MESH,
        )

    y_up, y_down, y_far = mod(y + 1, 4), mod(y + 3, 4), mod(y + 2, 4)
    mine, other = zl * 4, (1 - zl) * 4
    lo, hi = pl.ds(0, 64), pl.ds(64, 64)

    def copy(c, n):
        if n == FAR:
            return to_y(py.at[c, y_far], far.at[c, 0], c, n, down)
        if n == FAR + 1:
            return to_y(py.at[c, 4 + y_far], far.at[c, 1], c, n, up)
        if n == NEAR:
            return to_y(py.at[c, y_down], near.at[c, 0], c, n, down)
        if n == NEAR + 1:
            return to_y(py.at[c, 4 + y_down], near.at[c, 1], c, n, down)
        if n == NEAR + 2:
            return to_y(py.at[c, y_up], near.at[c, 2], c, n, up)
        if n == NEAR + 3:
            return to_y(py.at[c, 4 + y_up], near.at[c, 3], c, n, up)
        if n == ZSUM:
            return to_y(py.at[c, other + y], zsum.at[c], c, n, zmate)
        if n == ZPRE:
            return to_y(pz.at[c, pl.ds(other, 4)], zpre.at[c], c, n, zmate)
        if n == ZFAR:
            return to_y(pz.at[c, mine + y_far, lo], zfar.at[c, 0], c, n, down)
        if n == ZFAR + 1:
            return to_y(pz.at[c, mine + y_far, hi], zfar.at[c, 1], c, n, up)
        if n == ZNEAR:
            return to_y(pz.at[c, mine + y_down, lo], znear.at[c, 0], c, n, down)
        if n == ZNEAR + 1:
            return to_y(pz.at[c, mine + y_down, hi], znear.at[c, 1], c, n, down)
        if n == ZNEAR + 2:
            return to_y(pz.at[c, mine + y_up, lo], znear.at[c, 2], c, n, up)
        return to_y(pz.at[c, mine + y_up, hi], znear.at[c, 3], c, n, up)

    def added(*parts):
        total = parts[0].astype(F32)
        for part in parts[1:]:
            total = total + part.astype(F32)
        return total.astype(BF)

    def stage_0(c):
        for n in (ZPRE, FAR, FAR + 1, NEAR + 1, NEAR + 2):
            copy(c, n).start()

    def stage_1(c):
        copy(c, FAR).wait_recv()
        py[c, y_down] = added(py[c, y_down], far[c, 0])
        copy(c, FAR + 1).wait_recv()
        py[c, 4 + y_up] = added(py[c, 4 + y_up], far[c, 1])
        copy(c, NEAR).start()
        copy(c, NEAR + 3).start()

    def stage_1b(c):
        copy(c, ZPRE).wait_recv()
        for d in (2, 1, 3, 0):
            to = mod(y + d, 4)
            pz[c, mine + to] = added(pz[c, mine + to], zpre[c, to])
        for n in (ZFAR, ZFAR + 1, ZNEAR + 1, ZNEAR + 2):
            copy(c, n).start()

    def stage_2(c):
        for n in range(4):
            copy(c, NEAR + n).wait_recv()
        there = 1 - zl
        py[c, other + y] = added(py[c, other + y], near[c, there], near[c, 2 + there])
        copy(c, ZSUM).start()
        copy(c, ZFAR).wait_recv()
        copy(c, ZFAR + 1).wait_recv()
        pz[c, mine + y_down, :64] = added(pz[c, mine + y_down, :64], zfar[c, 0])
        pz[c, mine + y_up, 64:] = added(pz[c, mine + y_up, 64:], zfar[c, 1])
        copy(c, ZNEAR).start()
        copy(c, ZNEAR + 3).start()

    def stage_3(c):
        rows = pl.ds(pl.multiple_of(c * CHUNK, CHUNK), CHUNK)
        for n in range(4):
            copy(c, ZNEAR + n).wait_recv()
        first = pl.ds(pl.multiple_of(c * CHUNK, 64), 64)
        second = pl.ds(pl.multiple_of(c * CHUNK + 64, 64), 64)
        out[first, :ZCOLS] = added(pz[c, mine + y, :64], znear[c, 0], znear[c, 2])
        out[second, :ZCOLS] = added(pz[c, mine + y, 64:], znear[c, 1], znear[c, 3])
        copy(c, ZSUM).wait_recv()
        out[rows, ZCOLS:] = added(py[c, mine + y], near[c, zl], near[c, 2 + zl], zsum[c])

    def early(c, _):
        attend(c, ((0, 0),), first=True)
        pl.when(c == 1)(gather_a0)
        pl.when(c == 2)(gather_a2)
        return 0

    waits = (gather_1, gather_2, gather_3, gather_4, gather_5, gather_6, gather_7)

    def one_chip(n, _):
        for at, gather in enumerate(waits):
            pl.when(n == at + 1)(gather)
        m = mod(n, 4)
        attend(0, ((div(n, 4), m + div(m, 2) - 2 * div(m, 3)),))
        return 0

    def step(n, _):
        c = div(n, 3)
        s = mod(n, 3)
        attend(c, ((div(s + 1, 2), mod(s + 1, 2)), (div(s, 2), 3 - mod(s, 2))))

        @pl.when(s == 1)
        def _():
            stage_1(c - 1)

        @pl.when(s == 2)
        def _():
            attend(c, ((1, 2),))
            stage_1b(c - 1)
            project(c)
            stage_0(c)
            stage_2(c - 1)
            pl.when(c >= 2)(lambda: stage_3(c - 2))

        return 0

    for load in loads:
        load.wait()
    mate_has(0, 0)
    lax.fori_loop(0, CHUNKS, early, 0)
    lax.fori_loop(1, 8, one_chip, 0)
    w_copy.wait()
    project(0)
    stage_0(0)
    lax.fori_loop(3, 3 * CHUNKS, step, 0)
    last = CHUNKS - 1
    stage_1(last)
    stage_3(last - 1)
    stage_1b(last)
    stage_2(last)
    stage_3(last)

    for n in range(len(kv_sends)):
        pltpu.make_async_remote_copy(
            src_ref=k, dst_ref=kv.at[blk, 0], send_sem=kv_send.at[n],
            recv_sem=kv_recv.at[blk, 0], device_id=(mate, head), device_id_type=MESH,
        ).wait_send()

    def sent(c, _):
        for n in range(14):
            copy(c, n).wait_send()
        return 0

    lax.fori_loop(0, CHUNKS, sent, 0)


def per_device(queries, keys, values, w_out, order):
    vmem = pl.BlockSpec(memory_space=pltpu.VMEM)
    return pl.pallas_call(
        kernel,
        out_shape=jax.ShapeDtypeStruct((CHUNK * CHUNKS, 1024), BF),
        in_specs=[pl.BlockSpec(memory_space=pltpu.SMEM)] + [pl.BlockSpec(memory_space=pl.ANY)] * 4,
        out_specs=vmem,
        scratch_shapes=[
            pltpu.VMEM((CHUNK * CHUNKS, 1024), BF),
            pltpu.VMEM((16, 2, 512, HD), BF),
            pltpu.VMEM((1024, 8192), BF),
            pltpu.VMEM((128, 128), BF),
            pltpu.VMEM((3, 128, 128), BF),
            pltpu.VMEM((CHUNKS, SUBS, 256, 1), F32),
            pltpu.VMEM((CHUNKS, SUBS, 256, 256), F32),
            pltpu.VMEM((CHUNK, 1024), BF),
            pltpu.VMEM((CHUNKS, 8, CHUNK, YCOLS), BF),
            pltpu.VMEM((CHUNKS, 8, CHUNK, ZCOLS), BF),
            pltpu.VMEM((CHUNKS, 2, CHUNK, YCOLS), BF),
            pltpu.VMEM((CHUNKS, 4, CHUNK, YCOLS), BF),
            pltpu.VMEM((CHUNKS, CHUNK, YCOLS), BF),
            pltpu.VMEM((CHUNKS, 4, CHUNK, ZCOLS), BF),
            pltpu.VMEM((CHUNKS, 2, 64, ZCOLS), BF),
            pltpu.VMEM((CHUNKS, 4, 64, ZCOLS), BF),
            pltpu.SemaphoreType.DMA((30,)),
            pltpu.SemaphoreType.DMA((16, 2)),
            pltpu.SemaphoreType.DMA((CHUNKS, 14)),
            pltpu.SemaphoreType.DMA((CHUNKS, 14)),
            pltpu.SemaphoreType.DMA,
            pltpu.SemaphoreType.DMA((3,)),
        ],
        compiler_params=pltpu.CompilerParams(
            collective_id=0, has_side_effects=True, vmem_limit_bytes=66_000_000
        ),
        name="prefill",
    )(order, queries, keys, values, w_out)


def solution(mesh):
    placed = (P("blk", "head"), P("blk", "head"), P("blk", "head"), P("head", None), P())
    return jax.shard_map(
        per_device, mesh=mesh, in_specs=placed, out_specs=P("blk", "head"), check_vma=False
    )
```

```python
import jax
import jax.numpy as jnp
from jax import lax
from jax.experimental import pallas as pl
from jax.experimental.pallas import tpu as pltpu
from jax.sharding import PartitionSpec as P

HD = 128
CHUNK = 128
CHUNKS = 4
HEADS = 8
SUBS = 4
ZCOLS = 384
YCOLS = 640
SCALE2 = HD**-0.5 * 1.4426950408889634
HIDDEN = -1e30
MESH = pl.DeviceIdType.MESH
BF = jnp.bfloat16
F32 = jnp.float32
FAR, NEAR, ZSUM, ZPRE, ZFAR, ZNEAR = 0, 2, 6, 7, 8, 10


def mod(a, n):
    return lax.rem(a, n)


def div(a, n):
    return lax.div(a, n)


def kernel(
    order, q_hbm, k, v, w_hbm, out,
    q, kv, w, eye, masks, top, acc, att,
    py, pz, far, near, zsum, zpre, zfar, znear,
    kv_send, kv_recv, send, recv, w_sem, in_sem,
):
    blk = lax.axis_index("blk")
    head = lax.axis_index("head")
    core = mod(blk, 2)
    x = mod(div(blk, 2), 4)
    zh = div(blk, 8)
    y = div(head, 2)
    zl = mod(head, 2)

    def block(dz, dx):
        return (mod(zh + dz, 2) * 4 + mod(x + dx, 4)) * 2 + core

    left, right, across = block(0, 3), block(0, 1), block(1, 0)
    mate = blk + 1 - 2 * core
    up = mod(y + 1, 4) * 2 + zl
    down = mod(y + 3, 4) * 2 + zl
    zmate = head + 1 - 2 * zl

    loads = [
        pltpu.make_async_copy(src, dst, in_sem.at[n])
        for n, (src, dst) in enumerate(((q_hbm, q), (k, kv.at[blk, 0]), (v, kv.at[blk, 1])))
    ]
    for load in loads:
        load.start()
    barrier = pltpu.get_barrier_semaphore()
    for peer in (left, right, across, mate):
        pl.semaphore_signal(barrier, inc=1, device_id=(peer, head), device_id_type=MESH)
    for peer in (up, down, zmate):
        pl.semaphore_signal(barrier, inc=1, device_id=(blk, peer), device_id_type=MESH)
    pl.semaphore_wait(barrier, 7)

    w_copy = pltpu.make_async_copy(w_hbm, w, w_sem)

    kv_sends = []

    def pass_on(source, part, to, own=False):
        ref = (k, v)[part] if own else kv.at[source, part]
        copy = pltpu.make_async_remote_copy(
            src_ref=ref, dst_ref=kv.at[source, part],
            send_sem=kv_send.at[len(kv_sends)], recv_sem=kv_recv.at[source, part],
            device_id=(to, head), device_id_type=MESH,
        )
        kv_sends.append(0)
        copy.start()

    def arrived(source, part):
        pltpu.make_async_remote_copy(
            src_ref=kv.at[source, part], dst_ref=kv.at[source, part],
            send_sem=kv_send.at[0], recv_sem=kv_recv.at[source, part],
            device_id=(mate, head), device_id_type=MESH,
        ).wait_recv()

    def mate_has(dz, dx):
        source = block(dz, dx) + 1 - 2 * core
        arrived(source, 0)
        arrived(source, 1)

    for to in (across, right, left, mate):
        for part in (0, 1):
            pass_on(blk, part, to, own=True)
    w_copy.start()

    row = lax.broadcasted_iota(jnp.int32, (128, 128), 0)
    col = lax.broadcasted_iota(jnp.int32, (128, 128), 1)
    eye[...] = jnp.where(row == col, 1.0, 0.0).astype(BF)
    masks[0] = jnp.zeros((128, 128), BF)
    masks[1] = jnp.where(row > col, HIDDEN, 0.0).astype(BF)
    masks[2] = jnp.full((128, 128), HIDDEN, BF)

    def gather_a0():
        arrived(left, 0)
        pass_on(left, 0, right)
        arrived(across, 0)
        pass_on(across, 0, right)
        pass_on(across, 0, left)

    def gather_a2():
        arrived(right, 1)
        pass_on(right, 1, left)
        arrived(across, 1)
        pass_on(across, 1, right)
        pass_on(across, 1, left)
        arrived(right, 0)
        arrived(left, 1)
        for source in (right, left, across):
            for part in (0, 1):
                pass_on(source, part, mate)

    def gather_1():
        mate_has(0, 1)

    def gather_2():
        two, zleft = block(0, 2), block(1, 3)
        for part in (0, 1):
            arrived(two, part)
            pass_on(two, part, mate)
        arrived(zleft, 0)
        pass_on(zleft, 0, right)
        mate_has(0, 3)

    def gather_3():
        mate_has(0, 2)

    def gather_4():
        zleft, zright = block(1, 3), block(1, 1)
        arrived(zright, 1)
        pass_on(zright, 1, left)
        arrived(zleft, 1)
        arrived(zright, 0)
        for source in (zright, zleft):
            for part in (0, 1):
                pass_on(source, part, mate)
        mate_has(1, 0)

    def gather_5():
        mate_has(1, 1)

    def gather_6():
        ztwo = block(1, 2)
        for part in (0, 1):
            arrived(ztwo, part)
            pass_on(ztwo, part, mate)
        mate_has(1, 3)

    def gather_7():
        mate_has(1, 2)

    def attend(c, places, first=False):
        rows = pl.ds(pl.multiple_of(c * CHUNK, CHUNK), CHUNK)
        query_pos = 2 * order[2 * blk + div(c, 2)] + mod(c, 2)
        chips = [mod(zh + dz, 2) * 4 + mod(x + dx, 4) for dz, dx in places]
        key_rows, value_rows = [], []
        ones = jnp.ones((128, 128), BF)
        for chip in chips:
            for b in (2 * chip, 2 * chip + 1):
                for t in range(4):
                    key_pos = 2 * order[2 * b + t // 2] + t % 2
                    kind = (key_pos > query_pos).astype(jnp.int32) + (
                        key_pos >= query_pos
                    ).astype(jnp.int32)
                    part = slice(t * 128, (t + 1) * 128)
                    key_rows.append(jnp.concatenate([kv[b, 0, part, :], masks[kind]], axis=1))
                    value_rows.append(jnp.concatenate([kv[b, 1, part, :], ones], axis=1))
        key_tile = jnp.concatenate(key_rows, axis=0)
        value_tile = jnp.concatenate(value_rows, axis=0)
        scores = []
        for u in range(SUBS):
            q_rows = [
                jnp.concatenate([q[rows, h * HD : (h + 1) * HD], eye[...]], axis=1)
                for h in (2 * u, 2 * u + 1)
            ]
            scores.append(lax.dot_general(
                jnp.concatenate(q_rows, axis=0), key_tile,
                (((1,), (1,)), ((), ())), preferred_element_type=F32,
            ))
        weights = []
        for u, score in enumerate(scores):
            new = jnp.max(score, axis=1, keepdims=True) * SCALE2
            fade = None
            if not first:
                old = top[c, u]
                new = jnp.maximum(old, new)
                fade = jnp.exp2(old - new)
            top[c, u] = new
            weights.append((jnp.exp2(score * SCALE2 - new).astype(BF), fade))
        for u, (weight, fade) in enumerate(weights):
            part = jnp.dot(weight, value_tile, preferred_element_type=F32)
            acc[c, u] = part if first else acc[c, u] * fade + part

    def project(c):
        for u in range(SUBS):
            mean = (acc[c, u, :, :HD] / acc[c, u, :, HD:]).astype(BF)
            for h in range(2):
                at = (2 * u + h) * HD
                att[:, at : at + HD] = mean[h * CHUNK : (h + 1) * CHUNK]

        def one(i, _):
            to = mod(y + 2 + i, 4)
            columns = pl.ds(pl.multiple_of(to * 2048, 2048), 2048)
            part = jnp.dot(att[...], w[:, columns], preferred_element_type=F32).astype(BF)
            for z in range(2):
                pz[c, z * 4 + to] = part[:, z * 1024 : z * 1024 + ZCOLS]
                py[c, z * 4 + to] = part[:, z * 1024 + ZCOLS : (z + 1) * 1024]

            @pl.when(i == 1)
            def _():
                copy(c, FAR).start()
                copy(c, FAR + 1).start()

            @pl.when(i == 2)
            def _():
                copy(c, NEAR + 1).start()

            return 0

        lax.fori_loop(0, 4, one, 0)

    def to_y(src, dst, c, n, peer):
        return pltpu.make_async_remote_copy(
            src_ref=src, dst_ref=dst, send_sem=send.at[c, n], recv_sem=recv.at[c, n],
            device_id=(blk, peer), device_id_type=MESH,
        )

    y_up, y_down, y_far = mod(y + 1, 4), mod(y + 3, 4), mod(y + 2, 4)
    mine, other = zl * 4, (1 - zl) * 4
    lo, hi = pl.ds(0, 64), pl.ds(64, 64)

    def copy(c, n):
        if n == FAR:
            return to_y(py.at[c, y_far], far.at[c, 0], c, n, down)
        if n == FAR + 1:
            return to_y(py.at[c, 4 + y_far], far.at[c, 1], c, n, up)
        if n == NEAR:
            return to_y(py.at[c, y_down], near.at[c, 0], c, n, down)
        if n == NEAR + 1:
            return to_y(py.at[c, 4 + y_down], near.at[c, 1], c, n, down)
        if n == NEAR + 2:
            return to_y(py.at[c, y_up], near.at[c, 2], c, n, up)
        if n == NEAR + 3:
            return to_y(py.at[c, 4 + y_up], near.at[c, 3], c, n, up)
        if n == ZSUM:
            return to_y(py.at[c, other + y], zsum.at[c], c, n, zmate)
        if n == ZPRE:
            return to_y(pz.at[c, pl.ds(other, 4)], zpre.at[c], c, n, zmate)
        if n == ZFAR:
            return to_y(pz.at[c, mine + y_far, lo], zfar.at[c, 0], c, n, down)
        if n == ZFAR + 1:
            return to_y(pz.at[c, mine + y_far, hi], zfar.at[c, 1], c, n, up)
        if n == ZNEAR:
            return to_y(pz.at[c, mine + y_down, lo], znear.at[c, 0], c, n, down)
        if n == ZNEAR + 1:
            return to_y(pz.at[c, mine + y_down, hi], znear.at[c, 1], c, n, down)
        if n == ZNEAR + 2:
            return to_y(pz.at[c, mine + y_up, lo], znear.at[c, 2], c, n, up)
        return to_y(pz.at[c, mine + y_up, hi], znear.at[c, 3], c, n, up)

    def added(*parts):
        total = parts[0].astype(F32)
        for part in parts[1:]:
            total = total + part.astype(F32)
        return total.astype(BF)

    def stage_0(c):
        for n in (ZPRE, NEAR + 2):
            copy(c, n).start()

    def stage_1(c):
        copy(c, FAR).wait_recv()
        py[c, y_down] = added(py[c, y_down], far[c, 0])
        copy(c, FAR + 1).wait_recv()
        py[c, 4 + y_up] = added(py[c, 4 + y_up], far[c, 1])
        copy(c, NEAR).start()
        copy(c, NEAR + 3).start()

    def stage_1b(c):
        copy(c, ZPRE).wait_recv()
        for d in (2, 1, 3, 0):
            to = mod(y + d, 4)
            pz[c, mine + to] = added(pz[c, mine + to], zpre[c, to])
        for n in (ZFAR, ZFAR + 1, ZNEAR + 1, ZNEAR + 2):
            copy(c, n).start()

    def stage_2(c):
        for n in range(4):
            copy(c, NEAR + n).wait_recv()
        there = 1 - zl
        py[c, other + y] = added(py[c, other + y], near[c, there], near[c, 2 + there])
        copy(c, ZSUM).start()

    def stage_2z(c):
        copy(c, ZFAR).wait_recv()
        copy(c, ZFAR + 1).wait_recv()
        pz[c, mine + y_down, :64] = added(pz[c, mine + y_down, :64], zfar[c, 0])
        pz[c, mine + y_up, 64:] = added(pz[c, mine + y_up, 64:], zfar[c, 1])
        copy(c, ZNEAR).start()
        copy(c, ZNEAR + 3).start()

    def stage_3(c):
        rows = pl.ds(pl.multiple_of(c * CHUNK, CHUNK), CHUNK)
        for n in range(4):
            copy(c, ZNEAR + n).wait_recv()
        first = pl.ds(pl.multiple_of(c * CHUNK, 64), 64)
        second = pl.ds(pl.multiple_of(c * CHUNK + 64, 64), 64)
        out[first, :ZCOLS] = added(pz[c, mine + y, :64], znear[c, 0], znear[c, 2])
        out[second, :ZCOLS] = added(pz[c, mine + y, 64:], znear[c, 1], znear[c, 3])
        copy(c, ZSUM).wait_recv()
        out[rows, ZCOLS:] = added(py[c, mine + y], near[c, zl], near[c, 2 + zl], zsum[c])

    def early(c, _):
        attend(c, ((0, 0),), first=True)
        pl.when(c == 1)(gather_a0)
        pl.when(c == 2)(gather_a2)
        return 0

    waits = (gather_1, gather_2, gather_3, gather_4, gather_5, gather_6, gather_7)

    def one_chip(n, _):
        for at, gather in enumerate(waits):
            pl.when(n == at + 1)(gather)
        m = mod(n, 4)
        attend(0, ((div(n, 4), m + div(m, 2) - 2 * div(m, 3)),))
        return 0

    def step(n, _):
        c = div(n, 3)
        s = mod(n, 3)
        attend(c, ((div(s + 1, 2), mod(s + 1, 2)), (div(s, 2), 3 - mod(s, 2))))

        @pl.when((s == 0) & (c >= 2))
        def _():
            stage_2z(c - 2)

        @pl.when(s == 1)
        def _():
            stage_1(c - 1)

        @pl.when(s == 2)
        def _():
            attend(c, ((1, 2),))
            stage_1b(c - 1)
            project(c)
            stage_0(c)
            stage_2(c - 1)
            pl.when(c >= 2)(lambda: stage_3(c - 2))

        return 0

    for load in loads:
        load.wait()
    mate_has(0, 0)
    lax.fori_loop(0, CHUNKS, early, 0)
    lax.fori_loop(1, 8, one_chip, 0)
    w_copy.wait()
    project(0)
    stage_0(0)
    lax.fori_loop(3, 3 * CHUNKS, step, 0)
    last = CHUNKS - 1
    stage_2z(last - 1)
    stage_1(last)
    stage_1b(last)
    stage_2(last)
    stage_3(last - 1)
    stage_2z(last)
    stage_3(last)

    for n in range(len(kv_sends)):
        pltpu.make_async_remote_copy(
            src_ref=k, dst_ref=kv.at[blk, 0], send_sem=kv_send.at[n],
            recv_sem=kv_recv.at[blk, 0], device_id=(mate, head), device_id_type=MESH,
        ).wait_send()

    def sent(c, _):
        for n in range(14):
            copy(c, n).wait_send()
        return 0

    lax.fori_loop(0, CHUNKS, sent, 0)


def per_device(queries, keys, values, w_out, order):
    vmem = pl.BlockSpec(memory_space=pltpu.VMEM)
    return pl.pallas_call(
        kernel,
        out_shape=jax.ShapeDtypeStruct((CHUNK * CHUNKS, 1024), BF),
        in_specs=[pl.BlockSpec(memory_space=pltpu.SMEM)] + [pl.BlockSpec(memory_space=pl.ANY)] * 4,
        out_specs=vmem,
        scratch_shapes=[
            pltpu.VMEM((CHUNK * CHUNKS, 1024), BF),
            pltpu.VMEM((16, 2, 512, HD), BF),
            pltpu.VMEM((1024, 8192), BF),
            pltpu.VMEM((128, 128), BF),
            pltpu.VMEM((3, 128, 128), BF),
            pltpu.VMEM((CHUNKS, SUBS, 256, 1), F32),
            pltpu.VMEM((CHUNKS, SUBS, 256, 256), F32),
            pltpu.VMEM((CHUNK, 1024), BF),
            pltpu.VMEM((CHUNKS, 8, CHUNK, YCOLS), BF),
            pltpu.VMEM((CHUNKS, 8, CHUNK, ZCOLS), BF),
            pltpu.VMEM((CHUNKS, 2, CHUNK, YCOLS), BF),
            pltpu.VMEM((CHUNKS, 4, CHUNK, YCOLS), BF),
            pltpu.VMEM((CHUNKS, CHUNK, YCOLS), BF),
            pltpu.VMEM((CHUNKS, 4, CHUNK, ZCOLS), BF),
            pltpu.VMEM((CHUNKS, 2, 64, ZCOLS), BF),
            pltpu.VMEM((CHUNKS, 4, 64, ZCOLS), BF),
            pltpu.SemaphoreType.DMA((30,)),
            pltpu.SemaphoreType.DMA((16, 2)),
            pltpu.SemaphoreType.DMA((CHUNKS, 14)),
            pltpu.SemaphoreType.DMA((CHUNKS, 14)),
            pltpu.SemaphoreType.DMA,
            pltpu.SemaphoreType.DMA((3,)),
        ],
        compiler_params=pltpu.CompilerParams(
            collective_id=0, has_side_effects=True, vmem_limit_bytes=66_000_000
        ),
        name="prefill",
    )(order, queries, keys, values, w_out)


def solution(mesh):
    placed = (P("blk", "head"), P("blk", "head"), P("blk", "head"), P("head", None), P())
    return jax.shard_map(
        per_device, mesh=mesh, in_specs=placed, out_specs=P("blk", "head"), check_vma=False
    )
```

```python
import jax
import jax.numpy as jnp
from jax import lax
from jax.experimental import pallas as pl
from jax.experimental.pallas import tpu as pltpu
from jax.sharding import PartitionSpec as P

HD = 128
CHUNK = 128
CHUNKS = 4
HEADS = 8
SUBS = 4
ZCOLS = 384
YCOLS = 640
SCALE2 = HD**-0.5 * 1.4426950408889634
HIDDEN = -1e30
MESH = pl.DeviceIdType.MESH
BF = jnp.bfloat16
F32 = jnp.float32
FAR, NEAR, ZSUM, ZPRE, ZFAR, ZNEAR = 0, 2, 6, 7, 8, 10


def mod(a, n):
    return lax.rem(a, n)


def div(a, n):
    return lax.div(a, n)


def kernel(
    order, q_hbm, k, v, w_hbm, out,
    q, kv, w, eye, masks, top, acc, att,
    py, pz, far, near, zsum, zpre, zfar, znear,
    kv_send, kv_recv, send, recv, w_sem, in_sem,
):
    blk = lax.axis_index("blk")
    head = lax.axis_index("head")
    core = mod(blk, 2)
    x = mod(div(blk, 2), 4)
    zh = div(blk, 8)
    y = div(head, 2)
    zl = mod(head, 2)

    def block(dz, dx):
        return (mod(zh + dz, 2) * 4 + mod(x + dx, 4)) * 2 + core

    left, right, across = block(0, 3), block(0, 1), block(1, 0)
    mate = blk + 1 - 2 * core
    up = mod(y + 1, 4) * 2 + zl
    down = mod(y + 3, 4) * 2 + zl
    zmate = head + 1 - 2 * zl

    loads = [
        pltpu.make_async_copy(src, dst, in_sem.at[n])
        for n, (src, dst) in enumerate(((q_hbm, q), (k, kv.at[blk, 0]), (v, kv.at[blk, 1])))
    ]
    for load in loads:
        load.start()
    barrier = pltpu.get_barrier_semaphore()
    for peer in (left, right, across, mate):
        pl.semaphore_signal(barrier, inc=1, device_id=(peer, head), device_id_type=MESH)
    for peer in (up, down, zmate):
        pl.semaphore_signal(barrier, inc=1, device_id=(blk, peer), device_id_type=MESH)
    pl.semaphore_wait(barrier, 7)

    w_copy = pltpu.make_async_copy(w_hbm, w, w_sem)

    kv_sends = []

    def pass_on(source, part, to, own=False):
        ref = (k, v)[part] if own else kv.at[source, part]
        copy = pltpu.make_async_remote_copy(
            src_ref=ref, dst_ref=kv.at[source, part],
            send_sem=kv_send.at[len(kv_sends)], recv_sem=kv_recv.at[source, part],
            device_id=(to, head), device_id_type=MESH,
        )
        kv_sends.append(0)
        copy.start()

    def arrived(source, part):
        pltpu.make_async_remote_copy(
            src_ref=kv.at[source, part], dst_ref=kv.at[source, part],
            send_sem=kv_send.at[0], recv_sem=kv_recv.at[source, part],
            device_id=(mate, head), device_id_type=MESH,
        ).wait_recv()

    def mate_has(dz, dx):
        source = block(dz, dx) + 1 - 2 * core
        arrived(source, 0)
        arrived(source, 1)

    for to in (across, right, left, mate):
        for part in (0, 1):
            pass_on(blk, part, to, own=True)
    w_copy.start()

    row = lax.broadcasted_iota(jnp.int32, (128, 128), 0)
    col = lax.broadcasted_iota(jnp.int32, (128, 128), 1)
    eye[...] = jnp.where(row == col, 1.0, 0.0).astype(BF)
    masks[0] = jnp.zeros((128, 128), BF)
    masks[1] = jnp.where(row > col, HIDDEN, 0.0).astype(BF)
    masks[2] = jnp.full((128, 128), HIDDEN, BF)

    def gather_a0():
        arrived(left, 0)
        pass_on(left, 0, right)
        arrived(across, 0)
        pass_on(across, 0, right)
        pass_on(across, 0, left)

    def gather_a2():
        arrived(right, 1)
        pass_on(right, 1, left)
        arrived(across, 1)
        pass_on(across, 1, right)
        pass_on(across, 1, left)
        arrived(right, 0)
        arrived(left, 1)
        for source in (right, left, across):
            for part in (0, 1):
                pass_on(source, part, mate)

    def gather_1():
        mate_has(0, 1)

    def gather_2():
        two, zleft = block(0, 2), block(1, 3)
        for part in (0, 1):
            arrived(two, part)
            pass_on(two, part, mate)
        arrived(zleft, 0)
        pass_on(zleft, 0, right)
        mate_has(0, 3)

    def gather_3():
        mate_has(0, 2)

    def gather_4():
        zleft, zright = block(1, 3), block(1, 1)
        arrived(zright, 1)
        pass_on(zright, 1, left)
        arrived(zleft, 1)
        arrived(zright, 0)
        for source in (zright, zleft):
            for part in (0, 1):
                pass_on(source, part, mate)
        mate_has(1, 0)

    def gather_5():
        mate_has(1, 1)

    def gather_6():
        ztwo = block(1, 2)
        for part in (0, 1):
            arrived(ztwo, part)
            pass_on(ztwo, part, mate)
        mate_has(1, 3)

    def gather_7():
        mate_has(1, 2)

    def attend(c, places, first=False):
        rows = pl.ds(pl.multiple_of(c * CHUNK, CHUNK), CHUNK)
        query_pos = 2 * order[2 * blk + div(c, 2)] + mod(c, 2)
        chips = [mod(zh + dz, 2) * 4 + mod(x + dx, 4) for dz, dx in places]
        key_rows, value_rows = [], []
        ones = jnp.ones((128, 128), BF)
        for chip in chips:
            for b in (2 * chip, 2 * chip + 1):
                for t in range(4):
                    key_pos = 2 * order[2 * b + t // 2] + t % 2
                    kind = (key_pos > query_pos).astype(jnp.int32) + (
                        key_pos >= query_pos
                    ).astype(jnp.int32)
                    part = slice(t * 128, (t + 1) * 128)
                    key_rows.append(jnp.concatenate([kv[b, 0, part, :], masks[kind]], axis=1))
                    value_rows.append(jnp.concatenate([kv[b, 1, part, :], ones], axis=1))
        key_tile = jnp.concatenate(key_rows, axis=0)
        value_tile = jnp.concatenate(value_rows, axis=0)
        scores = []
        for u in range(SUBS):
            q_rows = [
                jnp.concatenate([q[rows, h * HD : (h + 1) * HD], eye[...]], axis=1)
                for h in (2 * u, 2 * u + 1)
            ]
            scores.append(lax.dot_general(
                jnp.concatenate(q_rows, axis=0), key_tile,
                (((1,), (1,)), ((), ())), preferred_element_type=F32,
            ))
        weights = []
        for u, score in enumerate(scores):
            new = jnp.max(score, axis=1, keepdims=True) * SCALE2
            fade = None
            if not first:
                old = top[c, u]
                new = jnp.maximum(old, new)
                fade = jnp.exp2(old - new)
            top[c, u] = new
            weights.append((jnp.exp2(score * SCALE2 - new).astype(BF), fade))
        for u, (weight, fade) in enumerate(weights):
            part = jnp.dot(weight, value_tile, preferred_element_type=F32)
            acc[c, u] = part if first else acc[c, u] * fade + part

    def project(c):
        for u in range(SUBS):
            mean = (acc[c, u, :, :HD] / acc[c, u, :, HD:]).astype(BF)
            for h in range(2):
                at = (2 * u + h) * HD
                att[:, at : at + HD] = mean[h * CHUNK : (h + 1) * CHUNK]

        def one(i, _):
            to = mod(y + 2 + i, 4)
            columns = pl.ds(pl.multiple_of(to * 2048, 2048), 2048)
            part = jnp.dot(att[...], w[:, columns], preferred_element_type=F32).astype(BF)
            for z in range(2):
                pz[c, z * 4 + to] = part[:, z * 1024 : z * 1024 + ZCOLS]
                py[c, z * 4 + to] = part[:, z * 1024 + ZCOLS : (z + 1) * 1024]

            @pl.when(i == 1)
            def _():
                copy(c, FAR).start()
                copy(c, FAR + 1).start()

            @pl.when(i == 2)
            def _():
                copy(c, NEAR + 1).start()

            @pl.when(i >= 1)
            def _():
                across_z(c, i - 1).start()

            return 0

        lax.fori_loop(0, 4, one, 0)

    def to_y(src, dst, c, n, peer):
        return pltpu.make_async_remote_copy(
            src_ref=src, dst_ref=dst, send_sem=send.at[c, n], recv_sem=recv.at[c, n],
            device_id=(blk, peer), device_id_type=MESH,
        )

    y_up, y_down, y_far = mod(y + 1, 4), mod(y + 3, 4), mod(y + 2, 4)
    mine, other = zl * 4, (1 - zl) * 4
    lo, hi = pl.ds(0, 64), pl.ds(64, 64)

    def copy(c, n):
        if n == FAR:
            return to_y(py.at[c, y_far], far.at[c, 0], c, n, down)
        if n == FAR + 1:
            return to_y(py.at[c, 4 + y_far], far.at[c, 1], c, n, up)
        if n == NEAR:
            return to_y(py.at[c, y_down], near.at[c, 0], c, n, down)
        if n == NEAR + 1:
            return to_y(py.at[c, 4 + y_down], near.at[c, 1], c, n, down)
        if n == NEAR + 2:
            return to_y(py.at[c, y_up], near.at[c, 2], c, n, up)
        if n == NEAR + 3:
            return to_y(py.at[c, 4 + y_up], near.at[c, 3], c, n, up)
        if n == ZSUM:
            return to_y(py.at[c, other + y], zsum.at[c], c, n, zmate)
        if n == ZFAR:
            return to_y(pz.at[c, mine + y_far, lo], zfar.at[c, 0], c, n, down)
        if n == ZFAR + 1:
            return to_y(pz.at[c, mine + y_far, hi], zfar.at[c, 1], c, n, up)
        if n == ZNEAR:
            return to_y(pz.at[c, mine + y_down, lo], znear.at[c, 0], c, n, down)
        if n == ZNEAR + 1:
            return to_y(pz.at[c, mine + y_down, hi], znear.at[c, 1], c, n, down)
        if n == ZNEAR + 2:
            return to_y(pz.at[c, mine + y_up, lo], znear.at[c, 2], c, n, up)
        return to_y(pz.at[c, mine + y_up, hi], znear.at[c, 3], c, n, up)

    def across_z(c, d):
        to = mod(y + 2 + d, 4)
        return to_y(pz.at[c, other + to], zpre.at[c, to], c, 14 + d, zmate)

    def added(*parts):
        total = parts[0].astype(F32)
        for part in parts[1:]:
            total = total + part.astype(F32)
        return total.astype(BF)

    def stage_0(c):
        across_z(c, 3).start()
        copy(c, NEAR + 2).start()

    def stage_1(c):
        copy(c, FAR).wait_recv()
        py[c, y_down] = added(py[c, y_down], far[c, 0])
        copy(c, FAR + 1).wait_recv()
        py[c, 4 + y_up] = added(py[c, 4 + y_up], far[c, 1])
        copy(c, NEAR).start()
        copy(c, NEAR + 3).start()

    def stage_1b(c):
        for d, sends in enumerate(((ZFAR, ZFAR + 1), (ZNEAR + 1,), (), (ZNEAR + 2,))):
            across_z(c, d).wait_recv()
            to = mod(y + 2 + d, 4)
            pz[c, mine + to] = added(pz[c, mine + to], zpre[c, to])
            for n in sends:
                copy(c, n).start()

    def stage_2(c):
        for n in range(4):
            copy(c, NEAR + n).wait_recv()
        there = 1 - zl
        py[c, other + y] = added(py[c, other + y], near[c, there], near[c, 2 + there])
        copy(c, ZSUM).start()

    def stage_2z(c):
        copy(c, ZFAR).wait_recv()
        copy(c, ZFAR + 1).wait_recv()
        pz[c, mine + y_down, :64] = added(pz[c, mine + y_down, :64], zfar[c, 0])
        pz[c, mine + y_up, 64:] = added(pz[c, mine + y_up, 64:], zfar[c, 1])
        copy(c, ZNEAR).start()
        copy(c, ZNEAR + 3).start()

    def stage_3(c):
        rows = pl.ds(pl.multiple_of(c * CHUNK, CHUNK), CHUNK)
        for n in range(4):
            copy(c, ZNEAR + n).wait_recv()
        first = pl.ds(pl.multiple_of(c * CHUNK, 64), 64)
        second = pl.ds(pl.multiple_of(c * CHUNK + 64, 64), 64)
        out[first, :ZCOLS] = added(pz[c, mine + y, :64], znear[c, 0], znear[c, 2])
        out[second, :ZCOLS] = added(pz[c, mine + y, 64:], znear[c, 1], znear[c, 3])
        copy(c, ZSUM).wait_recv()
        out[rows, ZCOLS:] = added(py[c, mine + y], near[c, zl], near[c, 2 + zl], zsum[c])

    def early(c, _):
        attend(c, ((0, 0),), first=True)
        pl.when(c == 1)(gather_a0)
        pl.when(c == 2)(gather_a2)
        return 0

    waits = (gather_1, gather_2, gather_3, gather_4, gather_5, gather_6, gather_7)

    def one_chip(n, _):
        for at, gather in enumerate(waits):
            pl.when(n == at + 1)(gather)
        m = mod(n, 4)
        attend(0, ((div(n, 4), m + div(m, 2) - 2 * div(m, 3)),))
        return 0

    def step(n, _):
        c = div(n, 3)
        s = mod(n, 3)
        attend(c, ((div(s + 1, 2), mod(s + 1, 2)), (div(s, 2), 3 - mod(s, 2))))

        @pl.when((s == 0) & (c >= 2))
        def _():
            stage_2z(c - 2)

        @pl.when(s == 1)
        def _():
            stage_1(c - 1)

        @pl.when(s == 2)
        def _():
            attend(c, ((1, 2),))
            stage_1b(c - 1)
            project(c)
            stage_0(c)
            stage_2(c - 1)
            pl.when(c >= 2)(lambda: stage_3(c - 2))

        return 0

    for load in loads:
        load.wait()
    mate_has(0, 0)
    lax.fori_loop(0, CHUNKS, early, 0)
    lax.fori_loop(1, 8, one_chip, 0)
    w_copy.wait()
    project(0)
    stage_0(0)
    lax.fori_loop(3, 3 * CHUNKS, step, 0)
    last = CHUNKS - 1
    stage_2z(last - 1)
    stage_1(last)
    stage_1b(last)
    stage_2(last)
    stage_3(last - 1)
    stage_2z(last)
    stage_3(last)

    for n in range(len(kv_sends)):
        pltpu.make_async_remote_copy(
            src_ref=k, dst_ref=kv.at[blk, 0], send_sem=kv_send.at[n],
            recv_sem=kv_recv.at[blk, 0], device_id=(mate, head), device_id_type=MESH,
        ).wait_send()

    def sent(c, _):
        for n in range(14):
            if n != ZPRE:
                copy(c, n).wait_send()
        for d in range(4):
            across_z(c, d).wait_send()
        return 0

    lax.fori_loop(0, CHUNKS, sent, 0)


def per_device(queries, keys, values, w_out, order):
    vmem = pl.BlockSpec(memory_space=pltpu.VMEM)
    return pl.pallas_call(
        kernel,
        out_shape=jax.ShapeDtypeStruct((CHUNK * CHUNKS, 1024), BF),
        in_specs=[pl.BlockSpec(memory_space=pltpu.SMEM)] + [pl.BlockSpec(memory_space=pl.ANY)] * 4,
        out_specs=vmem,
        scratch_shapes=[
            pltpu.VMEM((CHUNK * CHUNKS, 1024), BF),
            pltpu.VMEM((16, 2, 512, HD), BF),
            pltpu.VMEM((1024, 8192), BF),
            pltpu.VMEM((128, 128), BF),
            pltpu.VMEM((3, 128, 128), BF),
            pltpu.VMEM((CHUNKS, SUBS, 256, 1), F32),
            pltpu.VMEM((CHUNKS, SUBS, 256, 256), F32),
            pltpu.VMEM((CHUNK, 1024), BF),
            pltpu.VMEM((CHUNKS, 8, CHUNK, YCOLS), BF),
            pltpu.VMEM((CHUNKS, 8, CHUNK, ZCOLS), BF),
            pltpu.VMEM((CHUNKS, 2, CHUNK, YCOLS), BF),
            pltpu.VMEM((CHUNKS, 4, CHUNK, YCOLS), BF),
            pltpu.VMEM((CHUNKS, CHUNK, YCOLS), BF),
            pltpu.VMEM((CHUNKS, 4, CHUNK, ZCOLS), BF),
            pltpu.VMEM((CHUNKS, 2, 64, ZCOLS), BF),
            pltpu.VMEM((CHUNKS, 4, 64, ZCOLS), BF),
            pltpu.SemaphoreType.DMA((30,)),
            pltpu.SemaphoreType.DMA((16, 2)),
            pltpu.SemaphoreType.DMA((CHUNKS, 18)),
            pltpu.SemaphoreType.DMA((CHUNKS, 18)),
            pltpu.SemaphoreType.DMA,
            pltpu.SemaphoreType.DMA((3,)),
        ],
        compiler_params=pltpu.CompilerParams(
            collective_id=0, has_side_effects=True, vmem_limit_bytes=66_000_000
        ),
        name="prefill",
    )(order, queries, keys, values, w_out)


def solution(mesh):
    placed = (P("blk", "head"), P("blk", "head"), P("blk", "head"), P("head", None), P())
    return jax.shard_map(
        per_device, mesh=mesh, in_specs=placed, out_specs=P("blk", "head"), check_vma=False
    )
```
